128 devices in a mesh: dir: 32 (over y, z, core), near: 4 (over x).
Axes of the slice: x: 4, y: 4, z: 4, core: 2. Of those that a mesh axis runs over, the one named last changes fastest.
Arguments:
- currents: bfloat16 [4096, 128, 128], P(('dir', 'near')), may hold values from -6 to 6
- counts: int32 [128], replicated, may hold values from 0 to 4, as said below
- near_source: int32 [4096, 6], P(('dir', 'near')), may hold values from 0 to 4095, as said below
- near_blocks: bfloat16 [4096, 6, 128, 256], P(('dir', 'near')), may hold values from -0.15625 to 0.15625
- aggregate: bfloat16 [8, 1152, 256], replicated, may hold values from -0.125 to 0.125
- receive: bfloat16 [8, 128, 2304], replicated, may hold values from -0.125 to 0.125
- translations: bfloat16 [4, 3, 1152, 64, 128], P(None, None, ('dir', 'near')), may hold values from -0.3125 to 0.3125
- source_blocks: int32 [4, 3], replicated, may hold values from 0 to 3, as said below
Outputs:
- fields: bfloat16 [4096, 128, 128], P(('dir', 'near'))
The draws below stay inside these ranges and needn't reach their ends.
Inputs may be any that keep to these rules, and one draw needn't show every extreme that they name: `counts`: devices 2 m and 2 m + 1 of dir and near together (neighbours along near) own exactly 4 parents between them; some device owns 4 and its neighbour none. `near_source`: every entry names a live leaf slot on the device of its row or on a device next to it along near with the same dir index. `source_blocks`: each row names 3 different blocks.
All inputs are finite; a program needn't handle non-finite values.
Results may differ from the reference program's by a relative error of at most 0.005.
Values may be sent and summed in bfloat16 or wider, within the bound.
No kernel may reach another device: no remote copies, remote signals or barrier semaphores. Data moves between devices by JAX's collectives and lax.ppermute only.
A program may use at most 128 MiB of HBM per device.

```python
import jax
import jax.numpy as jnp
from jax import lax

P_SIZE = 128
R = 64
K = 1152
NEAR_PER = 6
PAR_SLOTS = 4
BLOCK = 64
PARENTS = 256
LEAF_SLOTS = 32
NBLK = 4
LIST = 3
N_NEAR = 4
DEVICES = 128


def owned_counts(key):
    pair_count = PARENTS // PAR_SLOTS
    first_share = jax.random.randint(jax.random.fold_in(key, 11), (pair_count,), 0, PAR_SLOTS + 1)
    chosen = jax.random.randint(jax.random.fold_in(key, 12), (), 0, pair_count)
    extreme = PAR_SLOTS * jax.random.randint(jax.random.fold_in(key, 13), (), 0, 2)
    first_share = jnp.where(jnp.arange(pair_count) == chosen, extreme, first_share)
    return jnp.stack([first_share, PAR_SLOTS - first_share], axis=1).reshape(-1).astype(jnp.int32)


def draw_counts(key, part):
    return owned_counts(key)


def draw_near_source(key, part):
    counts = owned_counts(key)
    devices = counts.shape[0]
    slot_rows = devices * LEAF_SLOTS
    home_device = jnp.arange(slot_rows, dtype=jnp.int32) // LEAF_SLOTS
    shifts = jnp.array([-1, 0, 1], jnp.int32)
    position = home_device % N_NEAR
    moved_position = position[:, None] + shifts[None, :]
    inside = (moved_position >= 0) & (moved_position < N_NEAR)
    target = jnp.clip(home_device[:, None] + shifts[None, :], 0, devices - 1)
    has_parents = counts[target] > 0
    allowed = inside & has_parents
    scores = jax.random.randint(jax.random.fold_in(key, 21), (slot_rows, NEAR_PER, 3), 0, 1024) * 4 + jnp.arange(3, dtype=jnp.int32)
    scores = jnp.where(allowed[:, None, :], scores, -1)
    picked = jnp.argmax(scores, axis=-1)
    chosen = jnp.take_along_axis(jnp.broadcast_to(target[:, None, :], scores.shape), picked[..., None], axis=-1)[..., 0]
    slot_limit = 8 * counts[chosen]
    slot_drawn = jax.random.randint(jax.random.fold_in(key, 22), (slot_rows, NEAR_PER), 0, slot_limit)
    return (chosen * LEAF_SLOTS + slot_drawn).astype(jnp.int32)


def draw_source_blocks(key, part):
    scores = jax.random.randint(jax.random.fold_in(key, 31), (NBLK, NBLK), 0, 4096) * NBLK + jnp.arange(NBLK, dtype=jnp.int32)[None, :]
    ranked = jnp.argsort(scores, axis=1)
    return ranked[:, :LIST].astype(jnp.int32)


def shard_levels(key, extent, pieces, smallest, top_value):
    gain, own = 1.0, jax.random.fold_in(key, 6)
    for dim, blocks in pieces:
        draws = jnp.exp(jax.random.uniform(jax.random.fold_in(own, dim), (blocks,), jnp.float32, smallest / len(pieces), top_value / len(pieces)))
        gain = gain * jnp.repeat(draws, extent[dim] // blocks).reshape([-1 if axis == dim else 1 for axis in range(len(extent))])
    return gain


def scatter_about(key, shape, width, reach, pieces=(), kind=jnp.bfloat16):
    gain = shard_levels(key, shape, pieces, -0.22, 0.18) if pieces else 1.0
    drawn = jax.random.normal(key, shape, jnp.float32) * width * gain
    return jnp.minimum(jnp.maximum(drawn, -reach), reach).astype(kind)


def setup_inputs(seed: int = 0) -> dict:
    arg_keys = jax.random.split(jax.random.key(seed), 9)
    currents = scatter_about(arg_keys[0], (DEVICES * LEAF_SLOTS, P_SIZE, 2 * R), 1.0, 6.0, ((0, 128),))
    counts = draw_counts(jax.random.fold_in(arg_keys[8], 71), 0)
    near_source = draw_near_source(jax.random.fold_in(arg_keys[8], 71), 0)
    near_blocks = scatter_about(arg_keys[3], (DEVICES * LEAF_SLOTS, NEAR_PER, P_SIZE, 2 * P_SIZE), (2 * P_SIZE * NEAR_PER) ** -0.5, 0.15625, ((0, 128),))
    aggregate = scatter_about(arg_keys[4], (8, K, 2 * P_SIZE), (16 * P_SIZE) ** -0.5, 0.125)
    receive = scatter_about(arg_keys[5], (8, P_SIZE, 2 * K), (2 * K) ** -0.5, 0.125)
    translations = scatter_about(arg_keys[6], (NBLK, LIST, K, BLOCK, 2 * BLOCK), (2 * BLOCK * LIST) ** -0.5, 0.3125, ((2, 128),))
    source_blocks = draw_source_blocks(jax.random.fold_in(arg_keys[8], 71), 0)
    return {"currents": currents, "counts": counts, "near_source": near_source, "near_blocks": near_blocks, "aggregate": aggregate, "receive": receive, "translations": translations, "source_blocks": source_blocks}


def turned(values):
    middle = values.shape[-1] // 2
    return jnp.concatenate([-values[..., middle:], values[..., :middle]], axis=-1)


def parent_positions(counts):
    range_ends = jnp.cumsum(counts).astype(jnp.int32)
    parent_ids = jnp.arange(PARENTS, dtype=jnp.int32)
    before = (range_ends[None, :] <= parent_ids[:, None]).astype(jnp.int32)
    owners = jnp.sum(before, axis=1).astype(jnp.int32)
    starts = jnp.sum(before * counts[None, :], axis=1).astype(jnp.int32)
    return (owners * PAR_SLOTS + parent_ids - starts).astype(jnp.int32)


def reference(currents, counts, near_source, near_blocks, aggregate, receive, translations, source_blocks):
    slots = parent_positions(counts)
    leaves = currents.reshape(-1, 8, P_SIZE, 2 * R)
    owned = leaves[slots]
    stacked = jnp.concatenate([owned, turned(owned)], axis=2)
    aggregate_wide = aggregate.astype(jnp.float32)

    def radiate(group_rows):
        return jnp.einsum("ckq,gcqr->gkr", aggregate_wide, group_rows.astype(jnp.float32)).astype(jnp.bfloat16)

    patterns = lax.map(radiate, stacked.reshape(-1, 8, 8, 2 * P_SIZE, 2 * R)).reshape(PARENTS, K, 2 * R)
    blocks = patterns.reshape(NBLK, BLOCK, K, 2 * R)
    with_turned = jnp.concatenate([blocks, turned(blocks)], axis=1)

    def translate(target):
        sources = with_turned[source_blocks[target]].astype(jnp.float32)
        operators = translations[target].astype(jnp.float32)
        return jnp.einsum("lkij,ljkr->ikr", operators, sources).astype(jnp.bfloat16)

    incoming = lax.map(translate, jnp.arange(NBLK, dtype=jnp.int32)).reshape(PARENTS, K, 2 * R)
    receive_wide = receive.astype(jnp.float32)

    def absorb(group_rows):
        doubled = jnp.concatenate([group_rows, turned(group_rows)], axis=1).astype(jnp.float32)
        return jnp.einsum("cpk,gkr->gcpr", receive_wide, doubled)

    far_field = lax.map(absorb, incoming.reshape(-1, 8, K, 2 * R)).reshape(PARENTS * 8, P_SIZE, 2 * R)
    leaf_ids = (slots[:, None] * 8 + jnp.arange(8, dtype=jnp.int32)[None, :]).reshape(-1).astype(jnp.int32)

    def nearby(indices):
        operators = near_blocks[indices].astype(jnp.float32)
        sources = currents[near_source[indices]]
        doubled = jnp.concatenate([sources, turned(sources)], axis=2).astype(jnp.float32)
        return jnp.einsum("genq,geqr->gnr", operators, doubled)

    near_field = lax.map(nearby, leaf_ids.reshape(-1, 64)).reshape(-1, P_SIZE, 2 * R)
    summed = (far_field + near_field).astype(jnp.bfloat16)
    return jnp.zeros(currents.shape, jnp.bfloat16).at[leaf_ids].set(summed)
```

```python
import numpy as np
import jax
import jax.numpy as jnp
from jax import lax
from jax.experimental import pallas as pl
from jax.experimental.pallas import tpu as pltpu
from jax.sharding import PartitionSpec as P

AXES = ("dir", "near")
MIB = 1 << 20


def turned(values):
    middle = values.shape[-1] // 2
    return jnp.concatenate([-values[..., middle:], values[..., :middle]], axis=-1)


def radiate_kernel(place_ref, currents_ref, aggregate_ref, out_ref, stacked_ref, rows_ref):
    children = aggregate_ref.shape[0]
    tile = aggregate_ref.shape[1]
    positions = stacked_ref.shape[2] // 128

    @pl.when(pl.program_id(0) == 0)
    def _():
        offset = place_ref[0]
        count = place_ref[1]
        for p in range(positions):
            slot = p - offset
            live = jnp.logical_and(slot >= 0, slot < count)
            row = jnp.clip(slot, 0, positions - 1) * children

            @pl.when(live)
            def _():
                for c in range(children):
                    v = currents_ref[row + c]
                    stacked_ref[c, 0:128, p * 128 : (p + 1) * 128] = v
                    stacked_ref[c, 128:256, p * 128 : (p + 1) * 128] = turned(v)

            @pl.when(jnp.logical_not(live))
            def _():
                stacked_ref[:, :, p * 128 : (p + 1) * 128] = jnp.zeros(
                    (children, 256, 128), jnp.bfloat16
                )

    total = jnp.dot(aggregate_ref[0], stacked_ref[0], preferred_element_type=jnp.float32)
    for c in range(1, children):
        total += jnp.dot(aggregate_ref[c], stacked_ref[c], preferred_element_type=jnp.float32)
    for p in range(positions):
        rows_ref[pl.ds(p, tile, stride=positions), :] = total[:, p * 128 : (p + 1) * 128]
    out_ref[...] = rows_ref[...].astype(jnp.bfloat16)


def radiate(place, currents, aggregate):
    children, directions, width = aggregate.shape
    positions = currents.shape[0] // children
    tile = 144
    return pl.pallas_call(
        radiate_kernel,
        grid_spec=pltpu.PrefetchScalarGridSpec(
            num_scalar_prefetch=1,
            grid=(directions // tile,),
            in_specs=[
                pl.BlockSpec(currents.shape, lambda i, _: (0, 0, 0)),
                pl.BlockSpec((children, tile, width), lambda i, _: (0, i, 0)),
            ],
            out_specs=pl.BlockSpec((tile * positions, 128), lambda i, _: (i, 0)),
            scratch_shapes=[
                pltpu.VMEM((children, width, positions * 128), jnp.bfloat16),
                pltpu.VMEM((tile * positions, 128), jnp.float32),
            ],
        ),
        out_shape=jax.ShapeDtypeStruct((directions * positions, 128), jnp.bfloat16),
        compiler_params=pltpu.CompilerParams(vmem_limit_bytes=32 * MIB),
        name="radiate",
    )(place, currents, aggregate)


def pair_rows(per_group, positions):
    pairs = 4
    select = np.zeros((per_group * pairs * positions, 2 * pairs * per_group * positions))
    for r in range(per_group):
        for pair in range(pairs):
            for p in range(positions):
                row = (r * pairs + pair) * positions + p
                for side in range(2):
                    select[row, ((2 * pair + side) * per_group + r) * positions + p] = 1.0
    return select


def translate_kernel(
    blocks_ref, rows_ref, translations_ref, select_ref, spread_ref, out_ref, values_ref, sums_ref
):
    block_count, list_length, per_group = translations_ref.shape[:3]
    block = translations_ref.shape[3]
    chunk = select_ref.shape[1]
    groups = rows_ref.shape[0] // chunk
    per_block = groups // block_count
    step = block // per_block
    for g in range(groups):
        picked = jnp.dot(
            select_ref[...],
            rows_ref[g * chunk : (g + 1) * chunk, :],
            preferred_element_type=jnp.float32,
        ).astype(jnp.bfloat16)
        other = turned(picked)
        b = g // per_block
        start = (g % per_block) * step
        for r in range(per_group):
            part = slice(r * step, (r + 1) * step)
            values_ref[b, r, start : start + step, :] = picked[part]
            values_ref[b, r, block + start : block + start + step, :] = other[part]
    for t in range(block_count):
        for r in range(per_group):
            total = jnp.dot(
                translations_ref[t, 0, r],
                values_ref[blocks_ref[t, 0], r],
                preferred_element_type=jnp.float32,
            )
            for e in range(1, list_length):
                total += jnp.dot(
                    translations_ref[t, e, r],
                    values_ref[blocks_ref[t, e], r],
                    preferred_element_type=jnp.float32,
                )
            total = total.astype(jnp.bfloat16)
            for q in range(per_block):
                sums_ref[t * per_block + q, r * step : (r + 1) * step, :] = total[
                    q * step : (q + 1) * step
                ]
    for g in range(groups):
        out_ref[g * chunk : (g + 1) * chunk, :] = jnp.dot(
            spread_ref[...], sums_ref[g], preferred_element_type=jnp.float32
        ).astype(jnp.bfloat16)


def translate(source_blocks, rows, translations, positions):
    block_count, _, per_group, block, doubled = translations.shape
    select = pair_rows(per_group, positions)
    groups = rows.shape[0] // select.shape[1]
    vmem = pl.BlockSpec(memory_space=pltpu.VMEM)
    return pl.pallas_call(
        translate_kernel,
        in_specs=[pl.BlockSpec(memory_space=pltpu.SMEM), vmem, vmem, vmem, vmem],
        out_specs=vmem,
        scratch_shapes=[
            pltpu.VMEM((block_count, per_group, doubled, 128), jnp.bfloat16),
            pltpu.VMEM((groups, select.shape[0], 128), jnp.bfloat16),
        ],
        out_shape=jax.ShapeDtypeStruct(rows.shape, jnp.bfloat16),
        compiler_params=pltpu.CompilerParams(vmem_limit_bytes=32 * MIB),
        name="translate",
    )(
        source_blocks,
        rows,
        translations,
        jnp.asarray(select, jnp.bfloat16),
        jnp.asarray(select.T, jnp.bfloat16),
    )


def near_kernel(source_ref, left_ref, own_ref, right_ref, blocks_ref, out_ref, window_ref):
    slots = own_ref.shape[0]
    unknowns = own_ref.shape[1]
    terms = blocks_ref.shape[1]
    leaf = pl.program_id(0)

    @pl.when(leaf == 0)
    def _():
        for part, ref in enumerate((left_ref, own_ref, right_ref)):

            def fill(i, carry, part=part, ref=ref):
                v = ref[i]
                window_ref[part * slots + i, 0:unknowns, :] = v
                window_ref[part * slots + i, unknowns : 2 * unknowns, :] = turned(v)
                return carry

            lax.fori_loop(0, slots, fill, 0)

    total = jnp.dot(
        blocks_ref[0, 0], window_ref[source_ref[leaf * terms]], preferred_element_type=jnp.float32
    )
    for e in range(1, terms):
        total += jnp.dot(
            blocks_ref[0, e],
            window_ref[source_ref[leaf * terms + e]],
            preferred_element_type=jnp.float32,
        )
    out_ref[0] = total


def near(source, left, own, right, blocks):
    slots, unknowns, channels = own.shape
    _, terms, _, doubled = blocks.shape
    whole = pl.BlockSpec(own.shape, lambda i, _: (0, 0, 0))
    return pl.pallas_call(
        near_kernel,
        grid_spec=pltpu.PrefetchScalarGridSpec(
            num_scalar_prefetch=1,
            grid=(slots,),
            in_specs=[
                whole,
                whole,
                whole,
                pl.BlockSpec((1, terms, unknowns, doubled), lambda i, _: (i, 0, 0, 0)),
            ],
            out_specs=pl.BlockSpec((1, unknowns, channels), lambda i, _: (i, 0, 0)),
            scratch_shapes=[pltpu.VMEM((3 * slots, doubled, channels), jnp.bfloat16)],
        ),
        out_shape=jax.ShapeDtypeStruct((slots, unknowns, channels), jnp.float32),
        compiler_params=pltpu.CompilerParams(vmem_limit_bytes=40 * MIB),
        name="near",
    )(source.reshape(-1), left, own, right, blocks)


def receive_kernel(place_ref, rows_ref, receive_ref, near_ref, out_ref, wide_ref, doubled_ref):
    octants = receive_ref.shape[0]
    unknowns = receive_ref.shape[1]
    directions = receive_ref.shape[2] // 2
    positions = doubled_ref.shape[1] // 128
    children = 8
    step = pl.program_id(0)
    offset = place_ref[0]
    count = place_ref[1]

    @pl.when(step == 0)
    def _():
        wide_ref[...] = rows_ref[...].astype(jnp.float32)
        for p in range(positions):
            v = wide_ref[pl.ds(p, directions, stride=positions), :].astype(jnp.bfloat16)
            doubled_ref[0:directions, p * 128 : (p + 1) * 128] = v
            doubled_ref[directions : 2 * directions, p * 128 : (p + 1) * 128] = turned(v)
        out_ref[...] = jnp.zeros(out_ref.shape, out_ref.dtype)

    lines = receive_ref[...].reshape(octants * unknowns, 2 * directions)
    far = jnp.dot(lines, doubled_ref[...], preferred_element_type=jnp.float32)
    for p in range(positions):
        slot = p - offset

        @pl.when(jnp.logical_and(slot >= 0, slot < count))
        def _():
            for c in range(octants):
                leaf = slot * children + step * octants + c
                part = far[c * unknowns : (c + 1) * unknowns, p * 128 : (p + 1) * 128]
                out_ref[leaf] = (part + near_ref[leaf]).astype(jnp.bfloat16)


def absorb(place, rows, receive, near_field):
    children, unknowns, doubled = receive.shape
    slots = near_field.shape[0]
    positions = slots // children
    octants = 2
    return pl.pallas_call(
        receive_kernel,
        grid_spec=pltpu.PrefetchScalarGridSpec(
            num_scalar_prefetch=1,
            grid=(children // octants,),
            in_specs=[
                pl.BlockSpec(rows.shape, lambda i, _: (0, 0)),
                pl.BlockSpec((octants, unknowns, doubled), lambda i, _: (i, 0, 0)),
                pl.BlockSpec(near_field.shape, lambda i, _: (0, 0, 0)),
            ],
            out_specs=pl.BlockSpec(near_field.shape, lambda i, _: (0, 0, 0)),
            scratch_shapes=[
                pltpu.VMEM(rows.shape, jnp.float32),
                pltpu.VMEM((doubled, positions * 128), jnp.bfloat16),
            ],
        ),
        out_shape=jax.ShapeDtypeStruct(near_field.shape, jnp.bfloat16),
        compiler_params=pltpu.CompilerParams(vmem_limit_bytes=40 * MIB),
        name="absorb",
    )(place, rows, receive, near_field)


def in_hbm(array):
    return pltpu.with_memory_space_constraint(array, pltpu.HBM)


def swap(rows, positions):
    channels = rows.shape[-1]
    shaped = rows.reshape(-1, positions, channels)
    return lax.all_to_all(shaped, AXES, 0, 0, tiled=True).reshape(-1, channels)


def body(
    currents, counts, near_source, near_blocks, aggregate, receive, translations, source_blocks
):
    device = lax.axis_index(AXES)
    slots, unknowns, channels = currents.shape
    positions = slots // aggregate.shape[0]
    own_count = counts[device]
    offset = jnp.where(device % 2 == 1, counts[device - device % 2], 0)
    place = jnp.stack([offset, own_count]).astype(jnp.int32)

    patterns = radiate(place, in_hbm(currents), in_hbm(aggregate))
    gathered = swap(patterns, positions)

    later, _ = lax.optimization_barrier((currents, patterns))
    count = lax.axis_size("near")
    left = lax.ppermute(later, "near", [(i, i + 1) for i in range(count - 1)])
    right = lax.ppermute(later, "near", [(i + 1, i) for i in range(count - 1)])
    gathered, left, right = lax.optimization_barrier((gathered, left, right))

    incoming = translate(source_blocks, gathered, translations, positions)
    returned = swap(incoming, positions)

    local = near_source - (device - 1) * slots
    local, _ = lax.optimization_barrier((local, incoming))
    near_field = near(local, left, in_hbm(currents), right, in_hbm(near_blocks))
    return absorb(place, returned, in_hbm(receive), near_field)


def solution(mesh):
    spread = P(AXES, None, None)
    return jax.shard_map(
        body,
        mesh=mesh,
        in_specs=(
            spread,
            P(),
            P(AXES, None),
            P(AXES, None, None, None),
            P(),
            P(),
            P(None, None, AXES, None, None),
            P(),
        ),
        out_specs=spread,
        check_vma=False,
    )
```

```python
import numpy as np
import jax
import jax.numpy as jnp
from jax import lax
from jax.experimental import pallas as pl
from jax.experimental.pallas import tpu as pltpu
from jax.sharding import PartitionSpec as P

AXES = ("dir", "near")
MIB = 1 << 20


def turned(values):
    middle = values.shape[-1] // 2
    return jnp.concatenate([-values[..., middle:], values[..., :middle]], axis=-1)


def quarter(v):
    lane = lax.broadcasted_iota(jnp.int32, (1, v.shape[-1]), 1)
    sign = jnp.where(lane < v.shape[-1] // 2, -1.0, 1.0).astype(v.dtype)
    return pltpu.roll(v, v.shape[-1] // 2, 1) * sign


def own_range(counts_ref):
    device = lax.axis_index("dir") * lax.axis_size("near") + lax.axis_index("near")
    odd = device % 2
    return odd * counts_ref[device - odd], counts_ref[device]


def radiate_kernel(counts_ref, currents_ref, aggregate_ref, out_ref, stacked_ref, rows_ref):
    children = aggregate_ref.shape[0]
    tile = aggregate_ref.shape[1]
    positions = stacked_ref.shape[2] // 128

    @pl.when(pl.program_id(0) == 0)
    def _():
        offset, count = own_range(counts_ref)
        for p in range(positions):
            slot = p - offset
            live = jnp.logical_and(slot >= 0, slot < count)
            row = jnp.clip(slot, 0, positions - 1) * children

            @pl.when(live)
            def _():
                for c in range(children):
                    v = currents_ref[row + c]
                    stacked_ref[c, 0:128, p * 128 : (p + 1) * 128] = v
                    stacked_ref[c, 128:256, p * 128 : (p + 1) * 128] = quarter(v)

            @pl.when(jnp.logical_not(live))
            def _():
                stacked_ref[:, :, p * 128 : (p + 1) * 128] = jnp.zeros(
                    (children, 256, 128), jnp.bfloat16
                )

    total = jnp.dot(aggregate_ref[0], stacked_ref[0], preferred_element_type=jnp.float32)
    for c in range(1, children):
        total += jnp.dot(aggregate_ref[c], stacked_ref[c], preferred_element_type=jnp.float32)
    for p in range(positions):
        rows_ref[pl.ds(p, tile, stride=positions), :] = total[:, p * 128 : (p + 1) * 128]
    out_ref[...] = rows_ref[...].astype(jnp.bfloat16)


def radiate(counts, currents, aggregate):
    children, directions, width = aggregate.shape
    positions = currents.shape[0] // children
    tile = 576
    return pl.pallas_call(
        radiate_kernel,
        grid_spec=pltpu.PrefetchScalarGridSpec(
            num_scalar_prefetch=1,
            grid=(directions // tile,),
            in_specs=[
                pl.BlockSpec(currents.shape, lambda i, _: (0, 0, 0)),
                pl.BlockSpec((children, tile, width), lambda i, _: (0, i, 0)),
            ],
            out_specs=pl.BlockSpec((tile * positions, 128), lambda i, _: (i, 0)),
            scratch_shapes=[
                pltpu.VMEM((children, width, positions * 128), jnp.bfloat16),
                pltpu.VMEM((tile * positions, 128), jnp.float32),
            ],
        ),
        out_shape=jax.ShapeDtypeStruct((directions * positions, 128), jnp.bfloat16),
        compiler_params=pltpu.CompilerParams(vmem_limit_bytes=32 * MIB),
        name="radiate",
    )(counts, currents, aggregate)


def pair_rows(per_group, positions):
    pairs = 4
    select = np.zeros((per_group * pairs * positions, 2 * pairs * per_group * positions))
    for r in range(per_group):
        for pair in range(pairs):
            for p in range(positions):
                row = (r * pairs + pair) * positions + p
                for side in range(2):
                    select[row, ((2 * pair + side) * per_group + r) * positions + p] = 1.0
    return select


def translate_kernel(
    blocks_ref, rows_ref, translations_ref, select_ref, spread_ref, out_ref, values_ref, sums_ref
):
    block_count, list_length, per_group = translations_ref.shape[:3]
    block = translations_ref.shape[3]
    chunk = select_ref.shape[1]
    groups = rows_ref.shape[0] // chunk
    per_block = groups // block_count
    step = block // per_block
    for g in range(groups):
        picked = jnp.dot(
            select_ref[...],
            rows_ref[g * chunk : (g + 1) * chunk, :],
            preferred_element_type=jnp.float32,
        ).astype(jnp.bfloat16)
        other = quarter(picked)
        b = g // per_block
        start = (g % per_block) * step
        for r in range(per_group):
            part = slice(r * step, (r + 1) * step)
            values_ref[b, r, start : start + step, :] = picked[part]
            values_ref[b, r, block + start : block + start + step, :] = other[part]
    for t in range(block_count):
        for r in range(per_group):
            total = jnp.dot(
                translations_ref[t, 0, r],
                values_ref[blocks_ref[t, 0], r],
                preferred_element_type=jnp.float32,
            )
            for e in range(1, list_length):
                total += jnp.dot(
                    translations_ref[t, e, r],
                    values_ref[blocks_ref[t, e], r],
                    preferred_element_type=jnp.float32,
                )
            total = total.astype(jnp.bfloat16)
            for q in range(per_block):
                sums_ref[t * per_block + q, r * step : (r + 1) * step, :] = total[
                    q * step : (q + 1) * step
                ]
    for g in range(groups):
        out_ref[g * chunk : (g + 1) * chunk, :] = jnp.dot(
            spread_ref[...], sums_ref[g], preferred_element_type=jnp.float32
        ).astype(jnp.bfloat16)


def translate(source_blocks, rows, translations, positions):
    block_count, _, per_group, block, doubled = translations.shape
    select = pair_rows(per_group, positions)
    groups = rows.shape[0] // select.shape[1]
    vmem = pl.BlockSpec(memory_space=pltpu.VMEM)
    return pl.pallas_call(
        translate_kernel,
        in_specs=[pl.BlockSpec(memory_space=pltpu.SMEM), vmem, vmem, vmem, vmem],
        out_specs=vmem,
        scratch_shapes=[
            pltpu.VMEM((block_count, per_group, doubled, 128), jnp.bfloat16),
            pltpu.VMEM((groups, select.shape[0], 128), jnp.bfloat16),
        ],
        out_shape=jax.ShapeDtypeStruct(rows.shape, jnp.bfloat16),
        compiler_params=pltpu.CompilerParams(vmem_limit_bytes=32 * MIB),
        name="translate",
    )(
        source_blocks,
        rows,
        translations,
        jnp.asarray(select, jnp.bfloat16),
        jnp.asarray(select.T, jnp.bfloat16),
    )


def near_kernel(source_ref, across_ref, own_ref, partner_ref, blocks_ref, out_ref, window_ref):
    slots = own_ref.shape[0]
    unknowns = own_ref.shape[1]
    leaves, terms = blocks_ref.shape[:2]
    first = pl.program_id(0) * leaves

    @pl.when(first == 0)
    def _():
        for part, ref in enumerate((across_ref, own_ref, partner_ref)):

            def fill(i, carry, part=part, ref=ref):
                for j in range(4):
                    v = ref[i * 4 + j]
                    row = part * slots + i * 4 + j
                    window_ref[row, 0:unknowns, :] = v
                    window_ref[row, unknowns : 2 * unknowns, :] = quarter(v)
                return carry

            lax.fori_loop(0, slots // 4, fill, 0)

    for i in range(leaves):
        sources = [source_ref[(first + i) * terms + e] for e in range(terms)]
        out_ref[i] = jnp.dot(
            jnp.concatenate([blocks_ref[i, e] for e in range(terms)], axis=1),
            jnp.concatenate([window_ref[source] for source in sources], axis=0),
            preferred_element_type=jnp.float32,
        )


def near(source, across, own, partner, blocks):
    slots, unknowns, channels = own.shape
    _, terms, _, doubled = blocks.shape
    leaves = 4
    whole = pl.BlockSpec(own.shape, lambda i, _: (0, 0, 0))
    return pl.pallas_call(
        near_kernel,
        grid_spec=pltpu.PrefetchScalarGridSpec(
            num_scalar_prefetch=1,
            grid=(slots // leaves,),
            in_specs=[
                whole,
                whole,
                whole,
                pl.BlockSpec((leaves, terms, unknowns, doubled), lambda i, _: (i, 0, 0, 0)),
            ],
            out_specs=pl.BlockSpec((leaves, unknowns, channels), lambda i, _: (i, 0, 0)),
            scratch_shapes=[pltpu.VMEM((3 * slots, doubled, channels), jnp.bfloat16)],
        ),
        out_shape=jax.ShapeDtypeStruct((slots, unknowns, channels), jnp.float32),
        compiler_params=pltpu.CompilerParams(vmem_limit_bytes=40 * MIB),
        cost_estimate=pl.CostEstimate(flops=10**10, transcendentals=0, bytes_accessed=2 * 10**7),
        name="near",
    )(source.reshape(-1), across, own, partner, blocks)


def receive_kernel(counts_ref, rows_ref, receive_ref, near_ref, out_ref, wide_ref, doubled_ref):
    octants = receive_ref.shape[0]
    unknowns = receive_ref.shape[1]
    directions = receive_ref.shape[2] // 2
    positions = doubled_ref.shape[1] // 128
    children = 8
    step = pl.program_id(0)
    offset, count = own_range(counts_ref)

    @pl.when(step == 0)
    def _():
        wide_ref[...] = rows_ref[...].astype(jnp.float32)
        for p in range(positions):
            v = wide_ref[pl.ds(p, directions, stride=positions), :].astype(jnp.bfloat16)
            doubled_ref[0:directions, p * 128 : (p + 1) * 128] = v
            doubled_ref[directions : 2 * directions, p * 128 : (p + 1) * 128] = quarter(v)
        out_ref[...] = jnp.zeros(out_ref.shape, out_ref.dtype)

    lines = receive_ref[...].reshape(octants * unknowns, 2 * directions)
    far = jnp.dot(lines, doubled_ref[...], preferred_element_type=jnp.float32)
    for p in range(positions):
        slot = p - offset

        @pl.when(jnp.logical_and(slot >= 0, slot < count))
        def _():
            for c in range(octants):
                leaf = slot * children + step * octants + c
                part = far[c * unknowns : (c + 1) * unknowns, p * 128 : (p + 1) * 128]
                out_ref[leaf] = (part + near_ref[leaf]).astype(jnp.bfloat16)


def absorb(counts, rows, receive, near_field):
    children, unknowns, doubled = receive.shape
    slots = near_field.shape[0]
    positions = slots // children
    octants = 4
    return pl.pallas_call(
        receive_kernel,
        grid_spec=pltpu.PrefetchScalarGridSpec(
            num_scalar_prefetch=1,
            grid=(children // octants,),
            in_specs=[
                pl.BlockSpec(rows.shape, lambda i, _: (0, 0)),
                pl.BlockSpec((octants, unknowns, doubled), lambda i, _: (i, 0, 0)),
                pl.BlockSpec(near_field.shape, lambda i, _: (0, 0, 0)),
            ],
            out_specs=pl.BlockSpec(near_field.shape, lambda i, _: (0, 0, 0)),
            scratch_shapes=[
                pltpu.VMEM(rows.shape, jnp.float32),
                pltpu.VMEM((doubled, positions * 128), jnp.bfloat16),
            ],
        ),
        out_shape=jax.ShapeDtypeStruct(near_field.shape, jnp.bfloat16),
        compiler_params=pltpu.CompilerParams(vmem_limit_bytes=40 * MIB),
        name="absorb",
    )(counts, rows, receive, near_field)


def in_hbm(array):
    return pltpu.with_memory_space_constraint(array, pltpu.HBM)


def swap(rows, positions):
    channels = rows.shape[-1]
    shaped = rows.reshape(-1, positions, channels)
    return lax.all_to_all(shaped, AXES, 0, 0, tiled=True).reshape(-1, channels)


def body(
    currents, counts, near_source, near_blocks, aggregate, receive, translations, source_blocks
):
    slots = currents.shape[0]
    positions = slots // aggregate.shape[0]
    device = lax.axis_index(AXES)
    local = near_source - (device - 1) * slots
    mirrored = local + 2 * slots - 2 * slots * (local // slots)
    local = jnp.where(device % 2 == 1, mirrored, local)
    count = lax.axis_size("near")
    inner = [(i, i + 1) for i in range(1, count - 1, 2)]
    outer = [(i, i + 1) for i in range(0, count, 2)]
    across = lax.ppermute(currents, "near", inner + [(j, i) for i, j in inner])
    partner = lax.ppermute(currents, "near", outer + [(j, i) for i, j in outer])

    patterns = radiate(counts, in_hbm(currents), in_hbm(aggregate))
    gathered = swap(patterns, positions)
    incoming = translate(source_blocks, gathered, translations, positions)
    returned = swap(incoming, positions)

    local, _ = lax.optimization_barrier((local, incoming))
    near_field = near(local, across, in_hbm(currents), partner, in_hbm(near_blocks))
    return absorb(counts, returned, in_hbm(receive), near_field)


def solution(mesh):
    spread = P(AXES, None, None)
    return jax.shard_map(
        body,
        mesh=mesh,
        in_specs=(
            spread,
            P(),
            P(AXES, None),
            P(AXES, None, None, None),
            P(),
            P(),
            P(None, None, AXES, None, None),
            P(),
        ),
        out_specs=spread,
        check_vma=False,
    )
```

```python
import numpy as np
import jax
import jax.numpy as jnp
from jax import lax
from jax.experimental import pallas as pl
from jax.experimental.pallas import tpu as pltpu
from jax.sharding import PartitionSpec as P

AXES = ("dir", "near")
MIB = 1 << 20


def turned(values):
    middle = values.shape[-1] // 2
    return jnp.concatenate([-values[..., middle:], values[..., :middle]], axis=-1)


def quarter(v):
    lane = lax.broadcasted_iota(jnp.int32, (1, v.shape[-1]), 1)
    sign = jnp.where(lane < v.shape[-1] // 2, -1.0, 1.0).astype(v.dtype)
    return pltpu.roll(v, v.shape[-1] // 2, 1) * sign


def own_range(counts_ref):
    device = lax.axis_index("dir") * lax.axis_size("near") + lax.axis_index("near")
    odd = device % 2
    return odd * counts_ref[device - odd], counts_ref[device]


def radiate_kernel(counts_ref, currents_ref, aggregate_ref, out_ref, stacked_ref, rows_ref):
    children = aggregate_ref.shape[0]
    tile = aggregate_ref.shape[1]
    positions = stacked_ref.shape[2] // 128

    @pl.when(pl.program_id(0) == 0)
    def _():
        offset, count = own_range(counts_ref)
        for p in range(positions):
            slot = p - offset
            live = jnp.logical_and(slot >= 0, slot < count)
            row = jnp.clip(slot, 0, positions - 1) * children

            @pl.when(live)
            def _():
                for c in range(children):
                    v = currents_ref[row + c]
                    stacked_ref[c, 0:128, p * 128 : (p + 1) * 128] = v
                    stacked_ref[c, 128:256, p * 128 : (p + 1) * 128] = quarter(v)

            @pl.when(jnp.logical_not(live))
            def _():
                stacked_ref[:, :, p * 128 : (p + 1) * 128] = jnp.zeros(
                    (children, 256, 128), jnp.bfloat16
                )

    total = jnp.dot(aggregate_ref[0], stacked_ref[0], preferred_element_type=jnp.float32)
    for c in range(1, children):
        total += jnp.dot(aggregate_ref[c], stacked_ref[c], preferred_element_type=jnp.float32)
    for p in range(positions):
        rows_ref[pl.ds(p, tile, stride=positions), :] = total[:, p * 128 : (p + 1) * 128]
    out_ref[...] = rows_ref[...].astype(jnp.bfloat16)


def radiate(counts, currents, aggregate):
    children, directions, width = aggregate.shape
    positions = currents.shape[0] // children
    tile = 576
    return pl.pallas_call(
        radiate_kernel,
        grid_spec=pltpu.PrefetchScalarGridSpec(
            num_scalar_prefetch=1,
            grid=(directions // tile,),
            in_specs=[
                pl.BlockSpec(currents.shape, lambda i, _: (0, 0, 0)),
                pl.BlockSpec((children, tile, width), lambda i, _: (0, i, 0)),
            ],
            out_specs=pl.BlockSpec((tile * positions, 128), lambda i, _: (i, 0)),
            scratch_shapes=[
                pltpu.VMEM((children, width, positions * 128), jnp.bfloat16),
                pltpu.VMEM((tile * positions, 128), jnp.float32),
            ],
        ),
        out_shape=jax.ShapeDtypeStruct((directions * positions, 128), jnp.bfloat16),
        compiler_params=pltpu.CompilerParams(vmem_limit_bytes=32 * MIB),
        name="radiate",
    )(counts, currents, aggregate)


def pair_rows(per_group, positions):
    pairs = 4
    select = np.zeros((per_group * pairs * positions, 2 * pairs * per_group * positions))
    for r in range(per_group):
        for pair in range(pairs):
            for p in range(positions):
                row = (r * pairs + pair) * positions + p
                for side in range(2):
                    select[row, ((2 * pair + side) * per_group + r) * positions + p] = 1.0
    return select


def translate_kernel(
    blocks_ref, rows_ref, translations_ref, select_ref, spread_ref, out_ref, values_ref, sums_ref
):
    block_count, list_length, per_group = translations_ref.shape[:3]
    block = translations_ref.shape[3]
    chunk = select_ref.shape[1]
    groups = rows_ref.shape[0] // chunk
    per_block = groups // block_count
    step = block // per_block
    for g in range(groups):
        picked = jnp.dot(
            select_ref[...],
            rows_ref[g * chunk : (g + 1) * chunk, :],
            preferred_element_type=jnp.float32,
        ).astype(jnp.bfloat16)
        other = quarter(picked)
        b = g // per_block
        start = (g % per_block) * step
        for r in range(per_group):
            part = slice(r * step, (r + 1) * step)
            values_ref[b, r, start : start + step, :] = picked[part]
            values_ref[b, r, block + start : block + start + step, :] = other[part]
    for t in range(block_count):
        for r in range(per_group):
            total = jnp.dot(
                translations_ref[t, 0, r],
                values_ref[blocks_ref[t, 0], r],
                preferred_element_type=jnp.float32,
            )
            for e in range(1, list_length):
                total += jnp.dot(
                    translations_ref[t, e, r],
                    values_ref[blocks_ref[t, e], r],
                    preferred_element_type=jnp.float32,
                )
            total = total.astype(jnp.bfloat16)
            for q in range(per_block):
                sums_ref[t * per_block + q, r * step : (r + 1) * step, :] = total[
                    q * step : (q + 1) * step
                ]
    for g in range(groups):
        out_ref[g * chunk : (g + 1) * chunk, :] = jnp.dot(
            spread_ref[...], sums_ref[g], preferred_element_type=jnp.float32
        ).astype(jnp.bfloat16)


def translate(source_blocks, rows, translations, positions):
    block_count, _, per_group, block, doubled = translations.shape
    select = pair_rows(per_group, positions)
    groups = rows.shape[0] // select.shape[1]
    vmem = pl.BlockSpec(memory_space=pltpu.VMEM)
    return pl.pallas_call(
        translate_kernel,
        in_specs=[pl.BlockSpec(memory_space=pltpu.SMEM), vmem, vmem, vmem, vmem],
        out_specs=vmem,
        scratch_shapes=[
            pltpu.VMEM((block_count, per_group, doubled, 128), jnp.bfloat16),
            pltpu.VMEM((groups, select.shape[0], 128), jnp.bfloat16),
        ],
        out_shape=jax.ShapeDtypeStruct(rows.shape, jnp.bfloat16),
        compiler_params=pltpu.CompilerParams(vmem_limit_bytes=32 * MIB),
        name="translate",
    )(
        source_blocks,
        rows,
        translations,
        jnp.asarray(select, jnp.bfloat16),
        jnp.asarray(select.T, jnp.bfloat16),
    )


def widen_kernel(across_ref, own_ref, partner_ref, out_ref):
    slots, unknowns, _ = own_ref.shape
    for part, ref in enumerate((across_ref, own_ref, partner_ref)):

        def fill(i, carry, part=part, ref=ref):
            for j in range(4):
                v = ref[i * 4 + j]
                row = part * slots + i * 4 + j
                out_ref[row, 0:unknowns, :] = v
                out_ref[row, unknowns : 2 * unknowns, :] = quarter(v)
            return carry

        lax.fori_loop(0, slots // 4, fill, 0)


def widen(across, own, partner):
    slots, unknowns, channels = own.shape
    vmem = pl.BlockSpec(memory_space=pltpu.VMEM)
    return pl.pallas_call(
        widen_kernel,
        in_specs=[vmem, vmem, vmem],
        out_specs=vmem,
        out_shape=pltpu.VMEM((3 * slots, 2 * unknowns, channels), own.dtype),
        compiler_params=pltpu.CompilerParams(vmem_limit_bytes=40 * MIB),
        cost_estimate=pl.CostEstimate(flops=5 * 10**10, transcendentals=0, bytes_accessed=10**7),
        name="widen",
    )(across, own, partner)


def near_kernel(source_ref, window_ref, blocks_ref, receive_hbm, out_ref, receive_ref, sem):
    leaves, terms = blocks_ref.shape[:2]
    step = pl.program_id(0)
    fetch = pltpu.make_async_copy(receive_hbm, receive_ref, sem)

    @pl.when(step == 0)
    def _():
        fetch.start()

    for i in range(leaves):
        first = (step * leaves + i) * terms
        sources = [source_ref[first + e] for e in range(terms)]
        out_ref[i] = jnp.dot(
            jnp.concatenate([blocks_ref[i, e] for e in range(terms)], axis=1),
            jnp.concatenate([window_ref[source] for source in sources], axis=0),
            preferred_element_type=jnp.float32,
        )

    @pl.when(step == pl.num_programs(0) - 1)
    def _():
        fetch.wait()


def near(source, window, blocks, receive):
    slots, terms, unknowns, doubled = blocks.shape
    channels = window.shape[-1]
    leaves = 4
    return pl.pallas_call(
        near_kernel,
        grid_spec=pltpu.PrefetchScalarGridSpec(
            num_scalar_prefetch=1,
            grid=(slots // leaves,),
            in_specs=[
                pl.BlockSpec(memory_space=pltpu.VMEM),
                pl.BlockSpec((leaves, terms, unknowns, doubled), lambda i, _: (i, 0, 0, 0)),
                pl.BlockSpec(memory_space=pltpu.HBM),
            ],
            out_specs=[
                pl.BlockSpec((leaves, unknowns, channels), lambda i, _: (i, 0, 0)),
                pl.BlockSpec(memory_space=pltpu.VMEM),
            ],
            scratch_shapes=[pltpu.SemaphoreType.DMA],
        ),
        out_shape=[
            jax.ShapeDtypeStruct((slots, unknowns, channels), jnp.float32),
            pltpu.VMEM(receive.shape, receive.dtype),
        ],
        compiler_params=pltpu.CompilerParams(vmem_limit_bytes=40 * MIB),
        cost_estimate=pl.CostEstimate(flops=10**10, transcendentals=0, bytes_accessed=2 * 10**7),
        name="near",
    )(source.reshape(-1), window, blocks, receive)


def absorb_kernel(counts_ref, rows_ref, receive_ref, near_ref, out_ref, wide_ref, doubled_ref):
    children, unknowns, doubled = receive_ref.shape
    directions = doubled // 2
    positions = doubled_ref.shape[1] // 128
    octants = 2
    offset, count = own_range(counts_ref)
    wide_ref[...] = rows_ref[...].astype(jnp.float32)
    for p in range(positions):
        v = wide_ref[pl.ds(p, directions, stride=positions), :].astype(jnp.bfloat16)
        doubled_ref[0:directions, p * 128 : (p + 1) * 128] = v
        doubled_ref[directions:doubled, p * 128 : (p + 1) * 128] = quarter(v)
    for q in range(0, children, octants):
        lines = receive_ref[q : q + octants].reshape(octants * unknowns, doubled)
        far = jnp.dot(lines, doubled_ref[...], preferred_element_type=jnp.float32)
        for p in range(positions):
            slot = p - offset

            @pl.when(jnp.logical_and(slot >= 0, slot < count))
            def _():
                for c in range(octants):
                    leaf = slot * children + q + c
                    part = far[c * unknowns : (c + 1) * unknowns, p * 128 : (p + 1) * 128]
                    out_ref[leaf] = (part + near_ref[leaf]).astype(jnp.bfloat16)

    for slot in range(positions):

        @pl.when(slot >= count)
        def _():
            out_ref[slot * children : (slot + 1) * children] = jnp.zeros(
                (children, unknowns, 128), jnp.bfloat16
            )


def absorb(counts, rows, receive, near_field):
    _, _, doubled = receive.shape
    positions = near_field.shape[0] // receive.shape[0]
    vmem = pl.BlockSpec(memory_space=pltpu.VMEM)
    return pl.pallas_call(
        absorb_kernel,
        in_specs=[pl.BlockSpec(memory_space=pltpu.SMEM), vmem, vmem, vmem],
        out_specs=vmem,
        scratch_shapes=[
            pltpu.VMEM(rows.shape, jnp.float32),
            pltpu.VMEM((doubled, positions * 128), jnp.bfloat16),
        ],
        out_shape=jax.ShapeDtypeStruct(near_field.shape, jnp.bfloat16),
        compiler_params=pltpu.CompilerParams(vmem_limit_bytes=40 * MIB),
        name="absorb",
    )(counts, rows, receive, near_field)


def in_hbm(array):
    return pltpu.with_memory_space_constraint(array, pltpu.HBM)


def swap(rows, positions):
    channels = rows.shape[-1]
    shaped = rows.reshape(-1, positions, channels)
    return lax.all_to_all(shaped, AXES, 0, 0, tiled=True).reshape(-1, channels)


def body(
    currents, counts, near_source, near_blocks, aggregate, receive, translations, source_blocks
):
    slots = currents.shape[0]
    positions = slots // aggregate.shape[0]
    device = lax.axis_index(AXES)
    local = near_source - (device - 1) * slots
    mirrored = local + 2 * slots - 2 * slots * (local // slots)
    local = jnp.where(device % 2 == 1, mirrored, local)
    count = lax.axis_size("near")
    inner = [(i, i + 1) for i in range(1, count - 1, 2)]
    outer = [(i, i + 1) for i in range(0, count, 2)]
    across = lax.ppermute(currents, "near", inner + [(j, i) for i, j in inner])
    partner = lax.ppermute(currents, "near", outer + [(j, i) for i, j in outer])

    patterns = radiate(in_hbm(counts), in_hbm(currents), in_hbm(aggregate))
    gathered = swap(patterns, positions)
    window = widen(across, currents, partner)
    gathered, window = lax.optimization_barrier((gathered, window))
    incoming = translate(source_blocks, gathered, translations, positions)
    returned = swap(incoming, positions)

    local, _ = lax.optimization_barrier((local, incoming))
    near_field, held = near(local, window, in_hbm(near_blocks), in_hbm(receive))
    return absorb(counts, returned, held, near_field)


def solution(mesh):
    spread = P(AXES, None, None)
    return jax.shard_map(
        body,
        mesh=mesh,
        in_specs=(
            spread,
            P(),
            P(AXES, None),
            P(AXES, None, None, None),
            P(),
            P(),
            P(None, None, AXES, None, None),
            P(),
        ),
        out_specs=spread,
        check_vma=False,
    )
```

```python
import numpy as np
import jax
import jax.numpy as jnp
from jax import lax
from jax.experimental import pallas as pl
from jax.experimental.pallas import tpu as pltpu
from jax.sharding import PartitionSpec as P

AXES = ("dir", "near")
MIB = 1 << 20


def quarter(v):
    lane = lax.broadcasted_iota(jnp.int32, (1, v.shape[-1]), 1)
    sign = jnp.where(lane < v.shape[-1] // 2, -1.0, 1.0).astype(v.dtype)
    return pltpu.roll(v, v.shape[-1] // 2, 1) * sign


def device_index():
    return lax.axis_index("dir") * lax.axis_size("near") + lax.axis_index("near")


def own_range(counts_ref):
    device = device_index()
    odd = device % 2
    return odd * counts_ref[device - odd], counts_ref[device]


def radiate_kernel(
    counts_ref, own_ref, moved_ref, aggregate_ref, out_hbm, stacked_ref, rows_ref, out_ref, sems
):
    children, directions, width = aggregate_ref.shape
    unknowns = width // 2
    share = stacked_ref.shape[1] // 128
    tiles = sems.shape[0]
    tile = directions // tiles
    device = device_index()
    odd = device % 2
    first = counts_ref[device - odd]
    for q in range(share):
        parent = share * odd + q
        lanes = slice(q * 128, (q + 1) * 128)
        mine = jnp.where(odd == 1, parent >= first, parent < first)
        slot = jnp.where(odd == 1, jnp.maximum(parent - first, 0), parent)
        arrived = jnp.where(odd == 1, q, jnp.clip(q - first, 0, share - 1))

        def place(ref, row, lanes=lanes):
            for c in range(children):
                v = ref[row * children + c]
                stacked_ref[c * width : c * width + unknowns, lanes] = v
                stacked_ref[c * width + unknowns : (c + 1) * width, lanes] = quarter(v)

        @pl.when(mine)
        def _():
            place(own_ref, slot)

        @pl.when(jnp.logical_not(mine))
        def _():
            place(moved_ref, arrived)

    stores = []
    for i in range(tiles):
        rows = slice(i * tile, (i + 1) * tile)
        total = jnp.dot(
            jnp.concatenate([aggregate_ref[c, rows, :] for c in range(children)], axis=1),
            stacked_ref[...],
            preferred_element_type=jnp.float32,
        )
        for q in range(share):
            rows_ref[pl.ds(q, tile, stride=share), :] = total[:, q * 128 : (q + 1) * 128]
        span = slice(i * tile * share, (i + 1) * tile * share)
        out_ref[span, :] = rows_ref[...].astype(jnp.bfloat16)
        store = pltpu.make_async_copy(out_ref.at[span], out_hbm.at[span], sems.at[i])
        store.start()
        stores.append(store)
    for store in stores:
        store.wait()


def radiate(counts, own, moved, aggregate):
    children, directions, width = aggregate.shape
    share = moved.shape[0] // children
    tiles = 4
    vmem = pl.BlockSpec(memory_space=pltpu.VMEM)
    return pl.pallas_call(
        radiate_kernel,
        in_specs=[pl.BlockSpec(memory_space=pltpu.SMEM), vmem, vmem, vmem],
        out_specs=pl.BlockSpec(memory_space=pltpu.HBM),
        scratch_shapes=[
            pltpu.VMEM((children * width, share * 128), jnp.bfloat16),
            pltpu.VMEM((directions // tiles * share, 128), jnp.float32),
            pltpu.VMEM((directions * share, 128), jnp.bfloat16),
            pltpu.SemaphoreType.DMA((tiles,)),
        ],
        out_shape=jax.ShapeDtypeStruct((directions * share, 128), jnp.bfloat16),
        compiler_params=pltpu.CompilerParams(vmem_limit_bytes=40 * MIB),
        name="radiate",
    )(counts, own, moved, aggregate)


def pair_rows(per_group, positions, copies):
    pairs = 4
    share = positions // (2 // copies)
    select = np.zeros((per_group * pairs * positions, 2 * pairs * per_group * share))
    for r in range(per_group):
        for pair in range(pairs):
            for p in range(positions):
                row = (r * pairs + pair) * positions + p
                for side in range(2) if copies == 2 else (p // share,):
                    column = ((2 * pair + side) * per_group + r) * share + p % share
                    select[row, column] = 1.0
    return select


def translate_kernel(
    blocks_ref, rows_ref, translations_ref, select_ref, spread_ref, out_hbm, values_ref, sums_ref,
    out_ref, sems,
):
    block_count, list_length, per_group = translations_ref.shape[:3]
    block = translations_ref.shape[3]
    chunk = select_ref.shape[1]
    wide = spread_ref.shape[0]
    groups = rows_ref.shape[0] // chunk
    per_block = groups // block_count
    step = block // per_block
    for g in range(groups):
        picked = jnp.dot(
            select_ref[...],
            rows_ref[g * chunk : (g + 1) * chunk, :],
            preferred_element_type=jnp.float32,
        ).astype(jnp.bfloat16)
        other = quarter(picked)
        b = g // per_block
        start = (g % per_block) * step
        for r in range(per_group):
            part = slice(r * step, (r + 1) * step)
            values_ref[b, r, start : start + step, :] = picked[part]
            values_ref[b, r, block + start : block + start + step, :] = other[part]
    stores = []
    for t in range(block_count):
        sources = [blocks_ref[t, e] for e in range(list_length)]
        for r in range(per_group):
            total = jnp.dot(
                jnp.concatenate([translations_ref[t, e, r] for e in range(list_length)], axis=1),
                jnp.concatenate([values_ref[source, r] for source in sources], axis=0),
                preferred_element_type=jnp.float32,
            )
            total = total.astype(jnp.bfloat16)
            for q in range(per_block):
                sums_ref[t * per_block + q, r * step : (r + 1) * step, :] = total[
                    q * step : (q + 1) * step
                ]
        for g in range(t * per_block, (t + 1) * per_block):
            out_ref[g * wide : (g + 1) * wide, :] = jnp.dot(
                spread_ref[...], sums_ref[g], preferred_element_type=jnp.float32
            ).astype(jnp.bfloat16)
        span = slice(t * per_block * wide, (t + 1) * per_block * wide)
        store = pltpu.make_async_copy(out_ref.at[span], out_hbm.at[span], sems.at[t])
        store.start()
        stores.append(store)
    for store in stores:
        store.wait()


def translate(source_blocks, rows, translations, positions):
    block_count, _, per_group, block, doubled = translations.shape
    select = pair_rows(per_group, positions, 1)
    spread = pair_rows(per_group, positions, 2).T
    groups = rows.shape[0] // select.shape[1]
    vmem = pl.BlockSpec(memory_space=pltpu.VMEM)
    return pl.pallas_call(
        translate_kernel,
        in_specs=[pl.BlockSpec(memory_space=pltpu.SMEM), vmem, vmem, vmem, vmem],
        out_specs=pl.BlockSpec(memory_space=pltpu.HBM),
        scratch_shapes=[
            pltpu.VMEM((block_count, per_group, doubled, 128), jnp.bfloat16),
            pltpu.VMEM((groups, select.shape[0], 128), jnp.bfloat16),
            pltpu.VMEM((groups * spread.shape[0], 128), jnp.bfloat16),
            pltpu.SemaphoreType.DMA((block_count,)),
        ],
        out_shape=jax.ShapeDtypeStruct((groups * spread.shape[0], 128), jnp.bfloat16),
        compiler_params=pltpu.CompilerParams(vmem_limit_bytes=32 * MIB),
        name="translate",
    )(
        source_blocks,
        rows,
        translations,
        jnp.asarray(select, jnp.bfloat16),
        jnp.asarray(spread, jnp.bfloat16),
    )


def widen_kernel(across_ref, own_ref, moved_ref, rest_ref, out_ref):
    unknowns = own_ref.shape[1]
    start = 0
    for ref in (across_ref, own_ref, moved_ref, rest_ref):

        def fill(i, carry, start=start, ref=ref):
            for j in range(4):
                v = ref[i * 4 + j]
                row = start + i * 4 + j
                out_ref[row, 0:unknowns, :] = v
                out_ref[row, unknowns : 2 * unknowns, :] = quarter(v)
            return carry

        lax.fori_loop(0, ref.shape[0] // 4, fill, 0)
        start += ref.shape[0]


def widen(across, own, moved, rest):
    slots, unknowns, channels = own.shape
    vmem = pl.BlockSpec(memory_space=pltpu.VMEM)
    return pl.pallas_call(
        widen_kernel,
        in_specs=[vmem] * 4,
        out_specs=vmem,
        out_shape=jax.ShapeDtypeStruct((3 * slots, 2 * unknowns, channels), own.dtype),
        compiler_params=pltpu.CompilerParams(vmem_limit_bytes=40 * MIB),
        cost_estimate=pl.CostEstimate(flops=5 * 10**10, transcendentals=0, bytes_accessed=10**7),
        name="widen",
    )(across, own, moved, rest)


def near_kernel(source_ref, window_ref, blocks_ref, out_ref):
    leaves, terms = blocks_ref.shape[:2]
    step = pl.program_id(0)
    for i in range(leaves):
        first = (step * leaves + i) * terms
        sources = [source_ref[first + e] for e in range(terms)]
        out_ref[i] = jnp.dot(
            jnp.concatenate([blocks_ref[i, e] for e in range(terms)], axis=1),
            jnp.concatenate([window_ref[source] for source in sources], axis=0),
            preferred_element_type=jnp.float32,
        )


def near(source, window, blocks):
    slots, terms, unknowns, doubled = blocks.shape
    channels = window.shape[-1]
    leaves = 4
    return pl.pallas_call(
        near_kernel,
        grid_spec=pltpu.PrefetchScalarGridSpec(
            num_scalar_prefetch=1,
            grid=(slots // leaves,),
            in_specs=[
                pl.BlockSpec(memory_space=pltpu.VMEM),
                pl.BlockSpec((leaves, terms, unknowns, doubled), lambda i, _: (i, 0, 0, 0)),
            ],
            out_specs=pl.BlockSpec((leaves, unknowns, channels), lambda i, _: (i, 0, 0)),
        ),
        out_shape=jax.ShapeDtypeStruct((slots, unknowns, channels), jnp.float32),
        compiler_params=pltpu.CompilerParams(vmem_limit_bytes=40 * MIB),
        cost_estimate=pl.CostEstimate(flops=10**10, transcendentals=0, bytes_accessed=2 * 10**7),
        name="near",
    )(source.reshape(-1), window, blocks)


def absorb_kernel(
    counts_ref, rows_ref, near_ref, receive_hbm, out_hbm, wide_ref, doubled_ref, receive_ref,
    fields_ref, fetch_sems, store_sems,
):
    children, unknowns, doubled = receive_ref.shape
    directions = doubled // 2
    positions = doubled_ref.shape[1] // 128
    steps = fetch_sems.shape[0]
    octants = children // steps
    parts = []
    for q in range(steps):
        span = slice(q * octants, (q + 1) * octants)
        part = pltpu.make_async_copy(receive_hbm.at[span], receive_ref.at[span], fetch_sems.at[q])
        part.start()
        parts.append(part)
    offset, count = own_range(counts_ref)
    for slot in range(positions):

        @pl.when(slot >= count)
        def _():
            fields_ref[slot * children : (slot + 1) * children] = jnp.zeros(
                (children, unknowns, 128), jnp.bfloat16
            )

    wide_ref[...] = rows_ref[...].astype(jnp.float32)
    for p in range(positions):
        v = wide_ref[pl.ds(p, directions, stride=positions), :].astype(jnp.bfloat16)
        doubled_ref[0:directions, p * 128 : (p + 1) * 128] = v
        doubled_ref[directions:doubled, p * 128 : (p + 1) * 128] = quarter(v)
    stores = []
    for q in range(steps):
        parts[q].wait()
        lines = receive_ref[q * octants : (q + 1) * octants].reshape(octants * unknowns, doubled)
        far = jnp.dot(lines, doubled_ref[...], preferred_element_type=jnp.float32)
        for p in range(positions):
            slot = p - offset

            @pl.when(jnp.logical_and(slot >= 0, slot < count))
            def _():
                for c in range(octants):
                    leaf = slot * children + q * octants + c
                    part = far[c * unknowns : (c + 1) * unknowns, p * 128 : (p + 1) * 128]
                    fields_ref[leaf] = (part + near_ref[leaf]).astype(jnp.bfloat16)

        for slot in range(positions):
            span = pl.ds(slot * children + q * octants, octants)
            store = pltpu.make_async_copy(
                fields_ref.at[span], out_hbm.at[span], store_sems.at[q, slot]
            )
            store.start()
            stores.append(store)
    for store in stores:
        store.wait()


def absorb(counts, rows, receive, near_field):
    children, _, doubled = receive.shape
    positions = near_field.shape[0] // children
    steps = 4
    vmem = pl.BlockSpec(memory_space=pltpu.VMEM)
    hbm = pl.BlockSpec(memory_space=pltpu.HBM)
    return pl.pallas_call(
        absorb_kernel,
        in_specs=[pl.BlockSpec(memory_space=pltpu.SMEM), vmem, vmem, hbm],
        out_specs=hbm,
        scratch_shapes=[
            pltpu.VMEM(rows.shape, jnp.float32),
            pltpu.VMEM((doubled, positions * 128), jnp.bfloat16),
            pltpu.VMEM(receive.shape, receive.dtype),
            pltpu.VMEM(near_field.shape, jnp.bfloat16),
            pltpu.SemaphoreType.DMA((steps,)),
            pltpu.SemaphoreType.DMA((steps, positions)),
        ],
        out_shape=jax.ShapeDtypeStruct(near_field.shape, jnp.bfloat16),
        compiler_params=pltpu.CompilerParams(vmem_limit_bytes=48 * MIB),
        name="absorb",
    )(counts, rows, near_field, receive)


def in_hbm(array):
    return pltpu.with_memory_space_constraint(array, pltpu.HBM)


def swap(rows, share):
    channels = rows.shape[-1]
    shaped = rows.reshape(-1, share, channels)
    return lax.all_to_all(shaped, AXES, 0, 0, tiled=True).reshape(-1, channels)


def body(
    currents, counts, near_source, near_blocks, aggregate, receive, translations, source_blocks
):
    slots = currents.shape[0]
    half = slots // 2
    positions = slots // aggregate.shape[0]
    device = lax.axis_index(AXES)
    odd = device % 2
    count = lax.axis_size("near")
    inner = [(i, i + 1) for i in range(1, count - 1, 2)]
    outer = [(i, i + 1) for i in range(0, count, 2)]
    inner += [(j, i) for i, j in inner]
    outer += [(j, i) for i, j in outer]
    excess = lax.dynamic_slice_in_dim(currents, (1 - odd) * half, half, 0)
    kept = lax.dynamic_slice_in_dim(currents, odd * half, half, 0)
    moved = lax.ppermute(excess, "near", outer)
    across = lax.ppermute(currents, "near", inner)
    rest = lax.ppermute(kept, "near", outer)

    patterns = radiate(in_hbm(counts), currents, moved, aggregate)
    gathered = swap(patterns, positions // 2)
    window = widen(across, currents, moved, rest)
    gathered, window = lax.optimization_barrier((gathered, window))
    incoming = translate(source_blocks, gathered, translations, positions)
    returned = swap(incoming, positions)

    local = near_source - (device - 1) * slots
    side, slot = local // slots, local % slots
    flipped = jnp.where(side == 0, 2 * slots + (slot + half) % slots, (2 - side) * slots + slot)
    local = jnp.where(odd == 1, flipped, local)
    local, _ = lax.optimization_barrier((local, incoming))
    near_field = near(local, window, in_hbm(near_blocks))
    return absorb(in_hbm(counts), returned, in_hbm(receive), near_field)


def solution(mesh):
    spread = P(AXES, None, None)
    return jax.shard_map(
        body,
        mesh=mesh,
        in_specs=(
            spread,
            P(),
            P(AXES, None),
            P(AXES, None, None, None),
            P(),
            P(),
            P(None, None, AXES, None, None),
            P(),
        ),
        out_specs=spread,
        check_vma=False,
    )
```

```python
import numpy as np
import jax
import jax.numpy as jnp
from jax import lax
from jax.experimental import pallas as pl
from jax.experimental.pallas import tpu as pltpu
from jax.sharding import PartitionSpec as P

AXES = ("dir", "near")
MIB = 1 << 20


def quarter(v):
    lane = lax.broadcasted_iota(jnp.int32, (1, v.shape[-1]), 1)
    sign = jnp.where(lane < v.shape[-1] // 2, -1.0, 1.0).astype(v.dtype)
    return pltpu.roll(v, v.shape[-1] // 2, 1) * sign


def own_range(counts_ref):
    device = lax.axis_index("dir") * lax.axis_size("near") + lax.axis_index("near")
    odd = device % 2
    return odd * counts_ref[device - odd], counts_ref[device]


def radiate_kernel(
    counts_ref, currents_hbm, aggregate_hbm, out_hbm, currents_ref, aggregate_ref, stacked_ref,
    rows_ref, out_ref, sems, store_sems,
):
    children, directions, width = aggregate_ref.shape
    unknowns = width // 2
    positions = stacked_ref.shape[1] // 128
    tiles = sems.shape[0] - 1
    tile = directions // tiles
    own = pltpu.make_async_copy(currents_hbm, currents_ref, sems.at[tiles])
    own.start()
    parts = []
    for i in range(tiles):
        rows = slice(i * tile, (i + 1) * tile)
        part = pltpu.make_async_copy(
            aggregate_hbm.at[:, rows, :], aggregate_ref.at[:, rows, :], sems.at[i]
        )
        part.start()
        parts.append(part)
    offset, count = own_range(counts_ref)
    own.wait()
    for p in range(positions):
        slot = p - offset
        live = jnp.logical_and(slot >= 0, slot < count)
        row = jnp.clip(slot, 0, positions - 1) * children
        lanes = slice(p * 128, (p + 1) * 128)

        @pl.when(live)
        def _():
            for c in range(children):
                v = currents_ref[row + c]
                stacked_ref[c * width : c * width + unknowns, lanes] = v
                stacked_ref[c * width + unknowns : (c + 1) * width, lanes] = quarter(v)

        @pl.when(jnp.logical_not(live))
        def _():
            stacked_ref[:, lanes] = jnp.zeros((children * width, 128), jnp.bfloat16)

    stores = []
    for i in range(tiles):
        parts[i].wait()
        rows = slice(i * tile, (i + 1) * tile)
        total = jnp.dot(
            jnp.concatenate([aggregate_ref[c, rows, :] for c in range(children)], axis=1),
            stacked_ref[...],
            preferred_element_type=jnp.float32,
        )
        for p in range(positions):
            rows_ref[pl.ds(p, tile, stride=positions), :] = total[:, p * 128 : (p + 1) * 128]
        span = slice(i * tile * positions, (i + 1) * tile * positions)
        out_ref[span, :] = rows_ref[...].astype(jnp.bfloat16)
        store = pltpu.make_async_copy(out_ref.at[span], out_hbm.at[span], store_sems.at[i])
        store.start()
        stores.append(store)
    for store in stores:
        store.wait()


def radiate(counts, currents, aggregate):
    children, directions, width = aggregate.shape
    positions = currents.shape[0] // children
    tiles = 4
    hbm = pl.BlockSpec(memory_space=pltpu.HBM)
    return pl.pallas_call(
        radiate_kernel,
        in_specs=[pl.BlockSpec(memory_space=pltpu.SMEM), hbm, hbm],
        out_specs=hbm,
        scratch_shapes=[
            pltpu.VMEM(currents.shape, currents.dtype),
            pltpu.VMEM(aggregate.shape, aggregate.dtype),
            pltpu.VMEM((children * width, positions * 128), jnp.bfloat16),
            pltpu.VMEM((directions // tiles * positions, 128), jnp.float32),
            pltpu.VMEM((directions * positions, 128), jnp.bfloat16),
            pltpu.SemaphoreType.DMA((tiles + 1,)),
            pltpu.SemaphoreType.DMA((tiles,)),
        ],
        out_shape=jax.ShapeDtypeStruct((directions * positions, 128), jnp.bfloat16),
        compiler_params=pltpu.CompilerParams(vmem_limit_bytes=40 * MIB),
        name="radiate",
    )(counts, currents, aggregate)


def pair_rows(per_group, positions):
    pairs = 4
    select = np.zeros((per_group * pairs * positions, 2 * pairs * per_group * positions))
    for r in range(per_group):
        for pair in range(pairs):
            for p in range(positions):
                row = (r * pairs + pair) * positions + p
                for side in range(2):
                    select[row, ((2 * pair + side) * per_group + r) * positions + p] = 1.0
    return select


def translate_kernel(
    blocks_ref, rows_ref, translations_ref, select_ref, spread_ref, out_hbm, values_ref, sums_ref,
    out_ref, sems,
):
    block_count, list_length, per_group = translations_ref.shape[:3]
    block = translations_ref.shape[3]
    chunk = select_ref.shape[1]
    groups = rows_ref.shape[0] // chunk
    per_block = groups // block_count
    step = block // per_block
    for g in range(groups):
        picked = jnp.dot(
            select_ref[...],
            rows_ref[g * chunk : (g + 1) * chunk, :],
            preferred_element_type=jnp.float32,
        ).astype(jnp.bfloat16)
        other = quarter(picked)
        b = g // per_block
        start = (g % per_block) * step
        for r in range(per_group):
            part = slice(r * step, (r + 1) * step)
            values_ref[b, r, start : start + step, :] = picked[part]
            values_ref[b, r, block + start : block + start + step, :] = other[part]
    stores = []
    for t in range(block_count):
        sources = [blocks_ref[t, e] for e in range(list_length)]
        for r in range(per_group):
            total = jnp.dot(
                jnp.concatenate([translations_ref[t, e, r] for e in range(list_length)], axis=1),
                jnp.concatenate([values_ref[source, r] for source in sources], axis=0),
                preferred_element_type=jnp.float32,
            )
            total = total.astype(jnp.bfloat16)
            for q in range(per_block):
                sums_ref[t * per_block + q, r * step : (r + 1) * step, :] = total[
                    q * step : (q + 1) * step
                ]
        for g in range(t * per_block, (t + 1) * per_block):
            out_ref[g * chunk : (g + 1) * chunk, :] = jnp.dot(
                spread_ref[...], sums_ref[g], preferred_element_type=jnp.float32
            ).astype(jnp.bfloat16)
        span = slice(t * per_block * chunk, (t + 1) * per_block * chunk)
        store = pltpu.make_async_copy(out_ref.at[span], out_hbm.at[span], sems.at[t])
        store.start()
        stores.append(store)
    for store in stores:
        store.wait()


def translate(source_blocks, rows, translations, positions):
    block_count, _, per_group, block, doubled = translations.shape
    select = pair_rows(per_group, positions)
    groups = rows.shape[0] // select.shape[1]
    vmem = pl.BlockSpec(memory_space=pltpu.VMEM)
    return pl.pallas_call(
        translate_kernel,
        in_specs=[pl.BlockSpec(memory_space=pltpu.SMEM), vmem, vmem, vmem, vmem],
        out_specs=pl.BlockSpec(memory_space=pltpu.HBM),
        scratch_shapes=[
            pltpu.VMEM((block_count, per_group, doubled, 128), jnp.bfloat16),
            pltpu.VMEM((groups, select.shape[0], 128), jnp.bfloat16),
            pltpu.VMEM(rows.shape, jnp.bfloat16),
            pltpu.SemaphoreType.DMA((block_count,)),
        ],
        out_shape=jax.ShapeDtypeStruct(rows.shape, jnp.bfloat16),
        compiler_params=pltpu.CompilerParams(vmem_limit_bytes=32 * MIB),
        name="translate",
    )(
        source_blocks,
        rows,
        translations,
        jnp.asarray(select, jnp.bfloat16),
        jnp.asarray(select.T, jnp.bfloat16),
    )


def near_kernel(source_ref, across_ref, own_ref, partner_ref, blocks_ref, out_ref, window_ref):
    slots = own_ref.shape[0]
    unknowns = own_ref.shape[1]
    leaves, terms = blocks_ref.shape[:2]
    first = pl.program_id(0) * leaves

    @pl.when(first == 0)
    def _():
        for part, ref in enumerate((across_ref, own_ref, partner_ref)):

            def fill(i, carry, part=part, ref=ref):
                for j in range(4):
                    v = ref[i * 4 + j]
                    row = part * slots + i * 4 + j
                    window_ref[row, 0:unknowns, :] = v
                    window_ref[row, unknowns : 2 * unknowns, :] = quarter(v)
                return carry

            lax.fori_loop(0, slots // 4, fill, 0)

    for i in range(leaves):
        sources = [source_ref[(first + i) * terms + e] for e in range(terms)]
        out_ref[i] = jnp.dot(
            jnp.concatenate([blocks_ref[i, e] for e in range(terms)], axis=1),
            jnp.concatenate([window_ref[source] for source in sources], axis=0),
            preferred_element_type=jnp.float32,
        )


def near(source, across, own, partner, blocks):
    slots, unknowns, channels = own.shape
    _, terms, _, doubled = blocks.shape
    leaves = 4
    whole = pl.BlockSpec(own.shape, lambda i, _: (0, 0, 0))
    return pl.pallas_call(
        near_kernel,
        grid_spec=pltpu.PrefetchScalarGridSpec(
            num_scalar_prefetch=1,
            grid=(slots // leaves,),
            in_specs=[
                whole,
                whole,
                whole,
                pl.BlockSpec((leaves, terms, unknowns, doubled), lambda i, _: (i, 0, 0, 0)),
            ],
            out_specs=pl.BlockSpec((leaves, unknowns, channels), lambda i, _: (i, 0, 0)),
            scratch_shapes=[pltpu.VMEM((3 * slots, doubled, channels), jnp.bfloat16)],
        ),
        out_shape=jax.ShapeDtypeStruct((slots, unknowns, channels), jnp.float32),
        compiler_params=pltpu.CompilerParams(vmem_limit_bytes=40 * MIB),
        cost_estimate=pl.CostEstimate(flops=10**10, transcendentals=0, bytes_accessed=2 * 10**7),
        name="near",
    )(source.reshape(-1), across, own, partner, blocks)


def absorb_kernel(
    counts_ref, rows_ref, near_ref, receive_hbm, out_hbm, wide_ref, doubled_ref, receive_ref,
    fields_ref, fetch_sems, store_sems,
):
    children, unknowns, doubled = receive_ref.shape
    directions = doubled // 2
    positions = doubled_ref.shape[1] // 128
    steps = fetch_sems.shape[0]
    octants = children // steps
    parts = []
    for q in range(steps):
        span = slice(q * octants, (q + 1) * octants)
        part = pltpu.make_async_copy(receive_hbm.at[span], receive_ref.at[span], fetch_sems.at[q])
        part.start()
        parts.append(part)
    offset, count = own_range(counts_ref)
    for slot in range(positions):

        @pl.when(slot >= count)
        def _():
            fields_ref[slot * children : (slot + 1) * children] = jnp.zeros(
                (children, unknowns, 128), jnp.bfloat16
            )

    wide_ref[...] = rows_ref[...].astype(jnp.float32)
    for p in range(positions):
        v = wide_ref[pl.ds(p, directions, stride=positions), :].astype(jnp.bfloat16)
        doubled_ref[0:directions, p * 128 : (p + 1) * 128] = v
        doubled_ref[directions:doubled, p * 128 : (p + 1) * 128] = quarter(v)
    stores = []
    for q in range(steps):
        parts[q].wait()
        lines = receive_ref[q * octants : (q + 1) * octants].reshape(octants * unknowns, doubled)
        far = jnp.dot(lines, doubled_ref[...], preferred_element_type=jnp.float32)
        for p in range(positions):
            slot = p - offset

            @pl.when(jnp.logical_and(slot >= 0, slot < count))
            def _():
                for c in range(octants):
                    leaf = slot * children + q * octants + c
                    part = far[c * unknowns : (c + 1) * unknowns, p * 128 : (p + 1) * 128]
                    fields_ref[leaf] = (part + near_ref[leaf]).astype(jnp.bfloat16)

        for slot in range(positions):
            span = pl.ds(slot * children + q * octants, octants)
            store = pltpu.make_async_copy(
                fields_ref.at[span], out_hbm.at[span], store_sems.at[q, slot]
            )
            store.start()
            stores.append(store)
    for store in stores:
        store.wait()


def absorb(counts, rows, receive, near_field):
    children, _, doubled = receive.shape
    positions = near_field.shape[0] // children
    steps = 4
    vmem = pl.BlockSpec(memory_space=pltpu.VMEM)
    hbm = pl.BlockSpec(memory_space=pltpu.HBM)
    return pl.pallas_call(
        absorb_kernel,
        in_specs=[pl.BlockSpec(memory_space=pltpu.SMEM), vmem, vmem, hbm],
        out_specs=hbm,
        scratch_shapes=[
            pltpu.VMEM(rows.shape, jnp.float32),
            pltpu.VMEM((doubled, positions * 128), jnp.bfloat16),
            pltpu.VMEM(receive.shape, receive.dtype),
            pltpu.VMEM(near_field.shape, jnp.bfloat16),
            pltpu.SemaphoreType.DMA((steps,)),
            pltpu.SemaphoreType.DMA((steps, positions)),
        ],
        out_shape=jax.ShapeDtypeStruct(near_field.shape, jnp.bfloat16),
        compiler_params=pltpu.CompilerParams(vmem_limit_bytes=48 * MIB),
        name="absorb",
    )(counts, rows, near_field, receive)


def in_hbm(array):
    return pltpu.with_memory_space_constraint(array, pltpu.HBM)


def swap(rows, positions):
    channels = rows.shape[-1]
    shaped = rows.reshape(-1, positions, channels)
    return lax.all_to_all(shaped, AXES, 0, 0, tiled=True).reshape(-1, channels)


def body(
    currents, counts, near_source, near_blocks, aggregate, receive, translations, source_blocks
):
    slots = currents.shape[0]
    positions = slots // aggregate.shape[0]
    device = lax.axis_index(AXES)
    local = near_source - (device - 1) * slots
    mirrored = local + 2 * slots - 2 * slots * (local // slots)
    local = jnp.where(device % 2 == 1, mirrored, local)
    count = lax.axis_size("near")
    inner = [(i, i + 1) for i in range(1, count - 1, 2)]
    outer = [(i, i + 1) for i in range(0, count, 2)]
    across = lax.ppermute(currents, "near", inner + [(j, i) for i, j in inner])
    partner = lax.ppermute(currents, "near", outer + [(j, i) for i, j in outer])

    patterns = radiate(in_hbm(counts), in_hbm(currents), in_hbm(aggregate))
    gathered = swap(patterns, positions)
    incoming = translate(source_blocks, gathered, translations, positions)
    returned = swap(incoming, positions)

    local, _ = lax.optimization_barrier((local, incoming))
    near_field = near(local, across, in_hbm(currents), partner, in_hbm(near_blocks))
    return absorb(in_hbm(counts), returned, in_hbm(receive), near_field)


def solution(mesh):
    spread = P(AXES, None, None)
    return jax.shard_map(
        body,
        mesh=mesh,
        in_specs=(
            spread,
            P(),
            P(AXES, None),
            P(AXES, None, None, None),
            P(),
            P(),
            P(None, None, AXES, None, None),
            P(),
        ),
        out_specs=spread,
        check_vma=False,
    )
```

```python
import numpy as np
import jax
import jax.numpy as jnp
from jax import lax
from jax.experimental import pallas as pl
from jax.experimental.pallas import tpu as pltpu
from jax.sharding import PartitionSpec as P

AXES = ("dir", "near")
MIB = 1 << 20
SPLITS = (288, 288, 288, 288)
SHARES = (2, 2, 4)


def quarter(v):
    lane = lax.broadcasted_iota(jnp.int32, (1, v.shape[-1]), 1)
    sign = jnp.where(lane < v.shape[-1] // 2, -1.0, 1.0).astype(v.dtype)
    return pltpu.roll(v, v.shape[-1] // 2, 1) * sign


def own_range(counts_ref):
    device = lax.axis_index("dir") * lax.axis_size("near") + lax.axis_index("near")
    odd = device % 2
    return odd * counts_ref[device - odd], counts_ref[device]


def radiate_kernel(
    counts_hbm, currents_hbm, aggregate_hbm, out_hbm, counts_ref, currents_ref, aggregate_ref,
    stacked_ref, rows_ref, out_ref, sems, store_sems,
):
    children, directions, width = aggregate_ref.shape
    unknowns = width // 2
    positions = stacked_ref.shape[1] // 128
    tiles = [slice(sum(SPLITS[:i]), sum(SPLITS[: i + 1])) for i in range(len(SPLITS))]
    table = pltpu.make_async_copy(counts_hbm, counts_ref, sems.at[len(tiles) + 1])
    table.start()
    own = pltpu.make_async_copy(currents_hbm, currents_ref, sems.at[len(tiles)])
    own.start()
    parts = []
    for i, rows in enumerate(tiles):
        part = pltpu.make_async_copy(
            aggregate_hbm.at[:, rows, :], aggregate_ref.at[:, rows, :], sems.at[i]
        )
        part.start()
        parts.append(part)
    table.wait()
    offset, count = own_range(counts_ref)
    own.wait()
    for p in range(positions):
        slot = p - offset
        live = jnp.logical_and(slot >= 0, slot < count)
        row = jnp.clip(slot, 0, positions - 1) * children
        lanes = slice(p * 128, (p + 1) * 128)

        @pl.when(live)
        def _():
            for c in range(children):
                v = currents_ref[row + c]
                stacked_ref[c * width : c * width + unknowns, lanes] = v
                stacked_ref[c * width + unknowns : (c + 1) * width, lanes] = quarter(v)

        @pl.when(jnp.logical_not(live))
        def _():
            stacked_ref[:, lanes] = jnp.zeros((children * width, 128), jnp.bfloat16)

    stores = []
    for i, rows in enumerate(tiles):
        parts[i].wait()
        tile = SPLITS[i]
        total = jnp.dot(
            jnp.concatenate([aggregate_ref[c, rows, :] for c in range(children)], axis=1),
            stacked_ref[...],
            preferred_element_type=jnp.float32,
        )
        for p in range(positions):
            rows_ref[pl.ds(p, tile, stride=positions), :] = total[:, p * 128 : (p + 1) * 128]
        span = slice(rows.start * positions, rows.stop * positions)
        out_ref[span, :] = rows_ref[0 : tile * positions, :].astype(jnp.bfloat16)
        store = pltpu.make_async_copy(out_ref.at[span], out_hbm.at[span], store_sems.at[i])
        store.start()
        stores.append(store)
    for store in stores:
        store.wait()


def radiate(counts, currents, aggregate):
    children, directions, width = aggregate.shape
    positions = currents.shape[0] // children
    tiles = len(SPLITS)
    hbm = pl.BlockSpec(memory_space=pltpu.HBM)
    return pl.pallas_call(
        radiate_kernel,
        in_specs=[hbm, hbm, hbm],
        out_specs=hbm,
        scratch_shapes=[
            pltpu.SMEM(counts.shape, counts.dtype),
            pltpu.VMEM(currents.shape, currents.dtype),
            pltpu.VMEM(aggregate.shape, aggregate.dtype),
            pltpu.VMEM((children * width, positions * 128), jnp.bfloat16),
            pltpu.VMEM((max(SPLITS) * positions, 128), jnp.float32),
            pltpu.VMEM((directions * positions, 128), jnp.bfloat16),
            pltpu.SemaphoreType.DMA((tiles + 2,)),
            pltpu.SemaphoreType.DMA((tiles,)),
        ],
        out_shape=jax.ShapeDtypeStruct((directions * positions, 128), jnp.bfloat16),
        compiler_params=pltpu.CompilerParams(vmem_limit_bytes=40 * MIB),
        name="radiate",
    )(counts, currents, aggregate)


def pair_rows(per_group, positions):
    pairs = 4
    select = np.zeros((per_group * pairs * positions, 2 * pairs * per_group * positions))
    for r in range(per_group):
        for pair in range(pairs):
            for p in range(positions):
                row = (r * pairs + pair) * positions + p
                for side in range(2):
                    select[row, ((2 * pair + side) * per_group + r) * positions + p] = 1.0
    return select


def translate_kernel(
    blocks_hbm, rows_ref, translations_ref, select_ref, spread_ref, out_hbm, blocks_ref, values_ref,
    sums_ref, out_ref, sems,
):
    table = pltpu.make_async_copy(blocks_hbm, blocks_ref, sems.at[0])
    table.start()
    block_count, list_length, per_group = translations_ref.shape[:3]
    block = translations_ref.shape[3]
    chunk = select_ref.shape[1]
    groups = rows_ref.shape[0] // chunk
    per_block = groups // block_count
    step = block // per_block
    for h in range(0, groups, 2):
        both = jnp.dot(
            select_ref[...],
            jnp.concatenate(
                [rows_ref[g * chunk : (g + 1) * chunk, :] for g in (h, h + 1)], axis=1
            ),
            preferred_element_type=jnp.float32,
        ).astype(jnp.bfloat16)
        for g in (h, h + 1):
            picked = both[:, (g - h) * 128 : (g - h + 1) * 128]
            other = quarter(picked)
            b = g // per_block
            start = (g % per_block) * step
            for r in range(per_group):
                part = slice(r * step, (r + 1) * step)
                values_ref[b, r, start : start + step, :] = picked[part]
                values_ref[b, r, block + start : block + start + step, :] = other[part]
    table.wait()
    stores = []
    for t in range(block_count):
        sources = [blocks_ref[t, e] for e in range(list_length)]
        for r in range(per_group):
            total = jnp.dot(
                jnp.concatenate([translations_ref[t, e, r] for e in range(list_length)], axis=1),
                jnp.concatenate([values_ref[source, r] for source in sources], axis=0),
                preferred_element_type=jnp.float32,
            )
            total = total.astype(jnp.bfloat16)
            for q in range(per_block):
                sums_ref[t * per_block + q, r * step : (r + 1) * step, :] = total[
                    q * step : (q + 1) * step
                ]
        for h in range(t * per_block, (t + 1) * per_block, 2):
            both = jnp.dot(
                spread_ref[...],
                jnp.concatenate([sums_ref[h], sums_ref[h + 1]], axis=1),
                preferred_element_type=jnp.float32,
            ).astype(jnp.bfloat16)
            for g in (h, h + 1):
                out_ref[g * chunk : (g + 1) * chunk, :] = both[:, (g - h) * 128 : (g - h + 1) * 128]
        span = slice(t * per_block * chunk, (t + 1) * per_block * chunk)
        store = pltpu.make_async_copy(out_ref.at[span], out_hbm.at[span], sems.at[t + 1])
        store.start()
        stores.append(store)
    for store in stores:
        store.wait()


def translate(source_blocks, rows, translations, positions):
    block_count, _, per_group, block, doubled = translations.shape
    select = pair_rows(per_group, positions)
    groups = rows.shape[0] // select.shape[1]
    vmem = pl.BlockSpec(memory_space=pltpu.VMEM)
    return pl.pallas_call(
        translate_kernel,
        in_specs=[pl.BlockSpec(memory_space=pltpu.HBM), vmem, vmem, vmem, vmem],
        out_specs=pl.BlockSpec(memory_space=pltpu.HBM),
        scratch_shapes=[
            pltpu.SMEM(source_blocks.shape, source_blocks.dtype),
            pltpu.VMEM((block_count, per_group, doubled, 128), jnp.bfloat16),
            pltpu.VMEM((groups, select.shape[0], 128), jnp.bfloat16),
            pltpu.VMEM(rows.shape, jnp.bfloat16),
            pltpu.SemaphoreType.DMA((block_count + 1,)),
        ],
        out_shape=jax.ShapeDtypeStruct(rows.shape, jnp.bfloat16),
        compiler_params=pltpu.CompilerParams(vmem_limit_bytes=32 * MIB),
        name="translate",
    )(
        source_blocks,
        rows,
        translations,
        jnp.asarray(select, jnp.bfloat16),
        jnp.asarray(select.T, jnp.bfloat16),
    )


def near_kernel(source_ref, across_ref, own_ref, partner_ref, blocks_ref, out_ref, window_ref):
    slots = own_ref.shape[0]
    unknowns = own_ref.shape[1]
    leaves, terms = blocks_ref.shape[:2]
    first = pl.program_id(0) * leaves

    @pl.when(first == 0)
    def _():
        for part, ref in enumerate((across_ref, own_ref, partner_ref)):

            def fill(i, carry, part=part, ref=ref):
                for j in range(4):
                    v = ref[i * 4 + j]
                    row = part * slots + i * 4 + j
                    window_ref[row, 0:unknowns, :] = v
                    window_ref[row, unknowns : 2 * unknowns, :] = quarter(v)
                return carry

            lax.fori_loop(0, slots // 4, fill, 0)

    for i in range(leaves):
        sources = [source_ref[(first + i) * terms + e] for e in range(terms)]
        out_ref[i] = jnp.dot(
            jnp.concatenate([blocks_ref[i, e] for e in range(terms)], axis=1),
            jnp.concatenate([window_ref[source] for source in sources], axis=0),
            preferred_element_type=jnp.float32,
        )


def near(source, across, own, partner, blocks):
    slots, unknowns, channels = own.shape
    _, terms, _, doubled = blocks.shape
    leaves = 4
    whole = pl.BlockSpec(own.shape, lambda i, _: (0, 0, 0))
    return pl.pallas_call(
        near_kernel,
        grid_spec=pltpu.PrefetchScalarGridSpec(
            num_scalar_prefetch=1,
            grid=(slots // leaves,),
            in_specs=[
                whole,
                whole,
                whole,
                pl.BlockSpec((leaves, terms, unknowns, doubled), lambda i, _: (i, 0, 0, 0)),
            ],
            out_specs=pl.BlockSpec((leaves, unknowns, channels), lambda i, _: (i, 0, 0)),
            scratch_shapes=[pltpu.VMEM((3 * slots, doubled, channels), jnp.bfloat16)],
        ),
        out_shape=jax.ShapeDtypeStruct((slots, unknowns, channels), jnp.float32),
        compiler_params=pltpu.CompilerParams(vmem_limit_bytes=40 * MIB),
        cost_estimate=pl.CostEstimate(flops=10**10, transcendentals=0, bytes_accessed=2 * 10**7),
        name="near",
    )(source.reshape(-1), across, own, partner, blocks)


def absorb_kernel(
    counts_hbm, rows_ref, near_ref, receive_hbm, out_hbm, counts_ref, wide_ref, doubled_ref,
    receive_ref, fields_ref, fetch_sems, store_sems,
):
    children, unknowns, doubled = receive_ref.shape
    directions = doubled // 2
    positions = doubled_ref.shape[1] // 128
    spans = [slice(sum(SHARES[:q]), sum(SHARES[: q + 1])) for q in range(len(SHARES))]
    table = pltpu.make_async_copy(counts_hbm, counts_ref, fetch_sems.at[len(SHARES)])
    table.start()
    parts = []
    for q, span in enumerate(spans):
        part = pltpu.make_async_copy(receive_hbm.at[span], receive_ref.at[span], fetch_sems.at[q])
        part.start()
        parts.append(part)
    wide_ref[...] = rows_ref[...].astype(jnp.float32)
    for p in range(positions):
        v = wide_ref[pl.ds(p, directions, stride=positions), :].astype(jnp.bfloat16)
        doubled_ref[0:directions, p * 128 : (p + 1) * 128] = v
        doubled_ref[directions:doubled, p * 128 : (p + 1) * 128] = quarter(v)
    table.wait()
    offset, count = own_range(counts_ref)
    for slot in range(positions):

        @pl.when(slot >= count)
        def _():
            fields_ref[slot * children : (slot + 1) * children] = jnp.zeros(
                (children, unknowns, 128), jnp.bfloat16
            )

    stores = []
    for q, octants in enumerate(SHARES):
        parts[q].wait()
        base = spans[q].start
        lines = receive_ref[spans[q]].reshape(octants * unknowns, doubled)
        far = jnp.dot(lines, doubled_ref[...], preferred_element_type=jnp.float32)
        for p in range(positions):
            slot = p - offset

            @pl.when(jnp.logical_and(slot >= 0, slot < count))
            def _():
                for c in range(octants):
                    leaf = slot * children + base + c
                    part = far[c * unknowns : (c + 1) * unknowns, p * 128 : (p + 1) * 128]
                    fields_ref[leaf] = (part + near_ref[leaf]).astype(jnp.bfloat16)

        for slot in range(positions):
            span = pl.ds(slot * children + base, octants)
            store = pltpu.make_async_copy(
                fields_ref.at[span], out_hbm.at[span], store_sems.at[q, slot]
            )
            store.start()
            stores.append(store)
    for store in stores:
        store.wait()


def absorb(counts, rows, receive, near_field):
    children, _, doubled = receive.shape
    positions = near_field.shape[0] // children
    steps = len(SHARES)
    vmem = pl.BlockSpec(memory_space=pltpu.VMEM)
    hbm = pl.BlockSpec(memory_space=pltpu.HBM)
    return pl.pallas_call(
        absorb_kernel,
        in_specs=[hbm, vmem, vmem, hbm],
        out_specs=hbm,
        scratch_shapes=[
            pltpu.SMEM(counts.shape, counts.dtype),
            pltpu.VMEM(rows.shape, jnp.float32),
            pltpu.VMEM((doubled, positions * 128), jnp.bfloat16),
            pltpu.VMEM(receive.shape, receive.dtype),
            pltpu.VMEM(near_field.shape, jnp.bfloat16),
            pltpu.SemaphoreType.DMA((steps + 1,)),
            pltpu.SemaphoreType.DMA((steps, positions)),
        ],
        out_shape=jax.ShapeDtypeStruct(near_field.shape, jnp.bfloat16),
        compiler_params=pltpu.CompilerParams(vmem_limit_bytes=48 * MIB),
        name="absorb",
    )(counts, rows, near_field, receive)


def in_hbm(array):
    return pltpu.with_memory_space_constraint(array, pltpu.HBM)


def swap(rows, positions):
    channels = rows.shape[-1]
    shaped = rows.reshape(-1, positions, channels)
    return lax.all_to_all(shaped, AXES, 0, 0, tiled=True).reshape(-1, channels)


def body(
    currents, counts, near_source, near_blocks, aggregate, receive, translations, source_blocks
):
    slots = currents.shape[0]
    positions = slots // aggregate.shape[0]
    device = lax.axis_index(AXES)
    local = near_source - (device - 1) * slots
    mirrored = local + 2 * slots - 2 * slots * (local // slots)
    local = jnp.where(device % 2 == 1, mirrored, local)
    count = lax.axis_size("near")
    inner = [(i, i + 1) for i in range(1, count - 1, 2)]
    outer = [(i, i + 1) for i in range(0, count, 2)]
    across = lax.ppermute(currents, "near", inner + [(j, i) for i, j in inner])
    partner = lax.ppermute(currents, "near", outer + [(j, i) for i, j in outer])

    patterns = radiate(in_hbm(counts), in_hbm(currents), in_hbm(aggregate))
    gathered = swap(patterns, positions)
    incoming = translate(in_hbm(source_blocks), gathered, translations, positions)
    returned = swap(incoming, positions)

    local, _ = lax.optimization_barrier((local, incoming))
    near_field = near(local, across, in_hbm(currents), partner, in_hbm(near_blocks))
    return absorb(in_hbm(counts), returned, in_hbm(receive), near_field)


def solution(mesh):
    spread = P(AXES, None, None)
    return jax.shard_map(
        body,
        mesh=mesh,
        in_specs=(
            spread,
            P(),
            P(AXES, None),
            P(AXES, None, None, None),
            P(),
            P(),
            P(None, None, AXES, None, None),
            P(),
        ),
        out_specs=spread,
        check_vma=False,
    )
```

```python
import numpy as np
import jax
import jax.numpy as jnp
from jax import lax
from jax.experimental import pallas as pl
from jax.experimental.pallas import tpu as pltpu
from jax.sharding import PartitionSpec as P

AXES = ("dir", "near")
MIB = 1 << 20
SPLITS = (288, 288, 288, 288)
SHARES = (2, 2, 4)
HELD = 2


def quarter(v):
    lane = lax.broadcasted_iota(jnp.int32, (1, v.shape[-1]), 1)
    sign = jnp.where(lane < v.shape[-1] // 2, -1.0, 1.0).astype(v.dtype)
    return pltpu.roll(v, v.shape[-1] // 2, 1) * sign


def own_range(counts_ref):
    device = lax.axis_index("dir") * lax.axis_size("near") + lax.axis_index("near")
    odd = device % 2
    return odd * counts_ref[device - odd], counts_ref[device]


def radiate_kernel(
    counts_hbm, currents_hbm, aggregate_hbm, out_hbm, counts_ref, currents_ref, aggregate_ref,
    stacked_ref, rows_ref, out_ref, sems, store_sems,
):
    children, directions, width = aggregate_ref.shape
    unknowns = width // 2
    positions = stacked_ref.shape[1] // 128
    tiles = [slice(sum(SPLITS[:i]), sum(SPLITS[: i + 1])) for i in range(len(SPLITS))]
    table = pltpu.make_async_copy(counts_hbm, counts_ref, sems.at[len(tiles) + 1])
    table.start()
    own = pltpu.make_async_copy(currents_hbm, currents_ref, sems.at[len(tiles)])
    own.start()
    parts = []
    for i, rows in enumerate(tiles):
        part = pltpu.make_async_copy(
            aggregate_hbm.at[:, rows, :], aggregate_ref.at[:, rows, :], sems.at[i]
        )
        part.start()
        parts.append(part)
    table.wait()
    offset, count = own_range(counts_ref)
    own.wait()
    for p in range(positions):
        slot = p - offset
        live = jnp.logical_and(slot >= 0, slot < count)
        row = jnp.clip(slot, 0, positions - 1) * children
        lanes = slice(p * 128, (p + 1) * 128)

        @pl.when(live)
        def _():
            for c in range(children):
                v = currents_ref[row + c]
                stacked_ref[c * width : c * width + unknowns, lanes] = v
                stacked_ref[c * width + unknowns : (c + 1) * width, lanes] = quarter(v)

        @pl.when(jnp.logical_not(live))
        def _():
            stacked_ref[:, lanes] = jnp.zeros((children * width, 128), jnp.bfloat16)

    stores = []
    for i, rows in enumerate(tiles):
        parts[i].wait()
        tile = SPLITS[i]
        total = jnp.dot(
            jnp.concatenate([aggregate_ref[c, rows, :] for c in range(children)], axis=1),
            stacked_ref[...],
            preferred_element_type=jnp.float32,
        )
        for p in range(positions):
            rows_ref[pl.ds(p, tile, stride=positions), :] = total[:, p * 128 : (p + 1) * 128]
        span = slice(rows.start * positions, rows.stop * positions)
        out_ref[span, :] = rows_ref[0 : tile * positions, :].astype(jnp.bfloat16)
        store = pltpu.make_async_copy(out_ref.at[span], out_hbm.at[span], store_sems.at[i])
        store.start()
        stores.append(store)
    for store in stores:
        store.wait()


def radiate(counts, currents, aggregate):
    children, directions, width = aggregate.shape
    positions = currents.shape[0] // children
    tiles = len(SPLITS)
    hbm = pl.BlockSpec(memory_space=pltpu.HBM)
    return pl.pallas_call(
        radiate_kernel,
        in_specs=[hbm, hbm, hbm],
        out_specs=hbm,
        scratch_shapes=[
            pltpu.SMEM(counts.shape, counts.dtype),
            pltpu.VMEM(currents.shape, currents.dtype),
            pltpu.VMEM(aggregate.shape, aggregate.dtype),
            pltpu.VMEM((children * width, positions * 128), jnp.bfloat16),
            pltpu.VMEM((max(SPLITS) * positions, 128), jnp.float32),
            pltpu.VMEM((directions * positions, 128), jnp.bfloat16),
            pltpu.SemaphoreType.DMA((tiles + 2,)),
            pltpu.SemaphoreType.DMA((tiles,)),
        ],
        out_shape=jax.ShapeDtypeStruct((directions * positions, 128), jnp.bfloat16),
        compiler_params=pltpu.CompilerParams(vmem_limit_bytes=28 * MIB),
        name="radiate",
    )(counts, currents, aggregate)


def pair_rows(per_group, positions):
    pairs = 4
    select = np.zeros((per_group * pairs * positions, 2 * pairs * per_group * positions))
    for r in range(per_group):
        for pair in range(pairs):
            for p in range(positions):
                row = (r * pairs + pair) * positions + p
                for side in range(2):
                    select[row, ((2 * pair + side) * per_group + r) * positions + p] = 1.0
    return select


def translate_kernel(
    blocks_hbm, rows_ref, translations_ref, select_ref, spread_ref, out_hbm, blocks_ref, values_ref,
    sums_ref, out_ref, sems,
):
    table = pltpu.make_async_copy(blocks_hbm, blocks_ref, sems.at[0])
    table.start()
    block_count, list_length, per_group = translations_ref.shape[:3]
    block = translations_ref.shape[3]
    chunk = select_ref.shape[1]
    groups = rows_ref.shape[0] // chunk
    per_block = groups // block_count
    step = block // per_block
    for h in range(0, groups, 2):
        both = jnp.dot(
            select_ref[...],
            jnp.concatenate(
                [rows_ref[g * chunk : (g + 1) * chunk, :] for g in (h, h + 1)], axis=1
            ),
            preferred_element_type=jnp.float32,
        ).astype(jnp.bfloat16)
        for g in (h, h + 1):
            picked = both[:, (g - h) * 128 : (g - h + 1) * 128]
            other = quarter(picked)
            b = g // per_block
            start = (g % per_block) * step
            for r in range(per_group):
                part = slice(r * step, (r + 1) * step)
                values_ref[b, r, start : start + step, :] = picked[part]
                values_ref[b, r, block + start : block + start + step, :] = other[part]
    table.wait()
    stores = []
    for t in range(block_count):
        sources = [blocks_ref[t, e] for e in range(list_length)]
        for r in range(per_group):
            total = jnp.dot(
                jnp.concatenate([translations_ref[t, e, r] for e in range(list_length)], axis=1),
                jnp.concatenate([values_ref[source, r] for source in sources], axis=0),
                preferred_element_type=jnp.float32,
            )
            total = total.astype(jnp.bfloat16)
            for q in range(per_block):
                sums_ref[t * per_block + q, r * step : (r + 1) * step, :] = total[
                    q * step : (q + 1) * step
                ]
        for h in range(t * per_block, (t + 1) * per_block, 2):
            both = jnp.dot(
                spread_ref[...],
                jnp.concatenate([sums_ref[h], sums_ref[h + 1]], axis=1),
                preferred_element_type=jnp.float32,
            ).astype(jnp.bfloat16)
            for g in (h, h + 1):
                out_ref[g * chunk : (g + 1) * chunk, :] = both[:, (g - h) * 128 : (g - h + 1) * 128]
        span = slice(t * per_block * chunk, (t + 1) * per_block * chunk)
        store = pltpu.make_async_copy(out_ref.at[span], out_hbm.at[span], sems.at[t + 1])
        store.start()
        stores.append(store)
    for store in stores:
        store.wait()


def translate(source_blocks, rows, translations, positions):
    block_count, _, per_group, block, doubled = translations.shape
    select = pair_rows(per_group, positions)
    groups = rows.shape[0] // select.shape[1]
    vmem = pl.BlockSpec(memory_space=pltpu.VMEM)
    return pl.pallas_call(
        translate_kernel,
        in_specs=[pl.BlockSpec(memory_space=pltpu.HBM), vmem, vmem, vmem, vmem],
        out_specs=pl.BlockSpec(memory_space=pltpu.HBM),
        scratch_shapes=[
            pltpu.SMEM(source_blocks.shape, source_blocks.dtype),
            pltpu.VMEM((block_count, per_group, doubled, 128), jnp.bfloat16),
            pltpu.VMEM((groups, select.shape[0], 128), jnp.bfloat16),
            pltpu.VMEM(rows.shape, jnp.bfloat16),
            pltpu.SemaphoreType.DMA((block_count + 1,)),
        ],
        out_shape=jax.ShapeDtypeStruct(rows.shape, jnp.bfloat16),
        compiler_params=pltpu.CompilerParams(vmem_limit_bytes=16 * MIB),
        name="translate",
    )(
        source_blocks,
        rows,
        translations,
        jnp.asarray(select, jnp.bfloat16),
        jnp.asarray(select.T, jnp.bfloat16),
    )


def near_kernel(
    source_ref, across_ref, own_ref, partner_ref, blocks_ref, receive_hbm, out_ref, held_ref,
    window_ref, sem,
):
    slots = own_ref.shape[0]
    unknowns = own_ref.shape[1]
    leaves, terms = blocks_ref.shape[:2]
    first = pl.program_id(0) * leaves
    hold = pltpu.make_async_copy(receive_hbm.at[0:HELD], held_ref, sem)

    @pl.when(first == 0)
    def _():
        hold.start()
        for part, ref in enumerate((across_ref, own_ref, partner_ref)):

            def fill(i, carry, part=part, ref=ref):
                for j in range(4):
                    v = ref[i * 4 + j]
                    row = part * slots + i * 4 + j
                    window_ref[row, 0:unknowns, :] = v
                    window_ref[row, unknowns : 2 * unknowns, :] = quarter(v)
                return carry

            lax.fori_loop(0, slots // 4, fill, 0)

    for i in range(leaves):
        sources = [source_ref[(first + i) * terms + e] for e in range(terms)]
        out_ref[i] = jnp.dot(
            jnp.concatenate([blocks_ref[i, e] for e in range(terms)], axis=1),
            jnp.concatenate([window_ref[source] for source in sources], axis=0),
            preferred_element_type=jnp.float32,
        ).astype(jnp.bfloat16)

    @pl.when(first == slots - leaves)
    def _():
        hold.wait()


def near(source, across, own, partner, blocks, receive):
    slots, unknowns, channels = own.shape
    _, terms, _, doubled = blocks.shape
    leaves = 4
    whole = pl.BlockSpec(own.shape, lambda i, _: (0, 0, 0))
    return pl.pallas_call(
        near_kernel,
        grid_spec=pltpu.PrefetchScalarGridSpec(
            num_scalar_prefetch=1,
            grid=(slots // leaves,),
            in_specs=[
                whole,
                whole,
                whole,
                pl.BlockSpec((leaves, terms, unknowns, doubled), lambda i, _: (i, 0, 0, 0)),
                pl.BlockSpec(memory_space=pltpu.HBM),
            ],
            out_specs=[
                pl.BlockSpec((leaves, unknowns, channels), lambda i, _: (i, 0, 0)),
                pl.BlockSpec(memory_space=pl.ANY),
            ],
            scratch_shapes=[
                pltpu.VMEM((3 * slots, doubled, channels), jnp.bfloat16),
                pltpu.SemaphoreType.DMA,
            ],
        ),
        out_shape=[
            jax.ShapeDtypeStruct((slots, unknowns, channels), jnp.bfloat16),
            jax.ShapeDtypeStruct((HELD,) + receive.shape[1:], receive.dtype),
        ],
        compiler_params=pltpu.CompilerParams(vmem_limit_bytes=28 * MIB),
        cost_estimate=pl.CostEstimate(flops=10**10, transcendentals=0, bytes_accessed=2 * 10**7),
        name="near",
    )(source.reshape(-1), across, own, partner, blocks, receive)


def absorb_kernel(
    counts_hbm, rows_ref, near_ref, held_ref, receive_hbm, out_hbm, counts_ref, wide_ref,
    doubled_ref, receive_ref, fields_ref, fetch_sems, store_sems,
):
    children, unknowns, doubled = receive_hbm.shape
    directions = doubled // 2
    positions = doubled_ref.shape[1] // 128
    spans = [slice(sum(SHARES[:q]), sum(SHARES[: q + 1])) for q in range(len(SHARES))]
    table = pltpu.make_async_copy(counts_hbm, counts_ref, fetch_sems.at[0])
    table.start()
    parts = [None]
    for q in range(1, len(SHARES)):
        span = slice(spans[q].start - HELD, spans[q].stop - HELD)
        part = pltpu.make_async_copy(
            receive_hbm.at[spans[q]], receive_ref.at[span], fetch_sems.at[q]
        )
        part.start()
        parts.append(part)
    wide_ref[...] = rows_ref[...].astype(jnp.float32)
    for p in range(positions):
        v = wide_ref[pl.ds(p, directions, stride=positions), :].astype(jnp.bfloat16)
        doubled_ref[0:directions, p * 128 : (p + 1) * 128] = v
        doubled_ref[directions:doubled, p * 128 : (p + 1) * 128] = quarter(v)
    table.wait()
    offset, count = own_range(counts_ref)
    for slot in range(positions):

        @pl.when(slot >= count)
        def _():
            fields_ref[slot * children : (slot + 1) * children] = jnp.zeros(
                (children, unknowns, 128), jnp.bfloat16
            )

    stores = []
    for q, octants in enumerate(SHARES):
        base = spans[q].start
        if q:
            parts[q].wait()
        held = receive_ref[base - HELD : base - HELD + octants] if q else held_ref[...]
        lines = held.reshape(octants * unknowns, doubled)
        far = jnp.dot(lines, doubled_ref[...], preferred_element_type=jnp.float32)
        for p in range(positions):
            slot = p - offset

            @pl.when(jnp.logical_and(slot >= 0, slot < count))
            def _():
                for c in range(octants):
                    leaf = slot * children + base + c
                    part = far[c * unknowns : (c + 1) * unknowns, p * 128 : (p + 1) * 128]
                    fields_ref[leaf] = (part + near_ref[leaf]).astype(jnp.bfloat16)

        for slot in range(positions):
            span = pl.ds(slot * children + base, octants)
            store = pltpu.make_async_copy(
                fields_ref.at[span], out_hbm.at[span], store_sems.at[q, slot]
            )
            store.start()
            stores.append(store)
    for store in stores:
        store.wait()


def absorb(counts, rows, held, receive, near_field):
    children, _, doubled = receive.shape
    positions = near_field.shape[0] // children
    steps = len(SHARES)
    vmem = pl.BlockSpec(memory_space=pltpu.VMEM)
    hbm = pl.BlockSpec(memory_space=pltpu.HBM)
    return pl.pallas_call(
        absorb_kernel,
        in_specs=[hbm, vmem, vmem, vmem, hbm],
        out_specs=hbm,
        scratch_shapes=[
            pltpu.SMEM(counts.shape, counts.dtype),
            pltpu.VMEM(rows.shape, jnp.float32),
            pltpu.VMEM((doubled, positions * 128), jnp.bfloat16),
            pltpu.VMEM((children - HELD,) + receive.shape[1:], receive.dtype),
            pltpu.VMEM(near_field.shape, jnp.bfloat16),
            pltpu.SemaphoreType.DMA((steps,)),
            pltpu.SemaphoreType.DMA((steps, positions)),
        ],
        out_shape=jax.ShapeDtypeStruct(near_field.shape, jnp.bfloat16),
        compiler_params=pltpu.CompilerParams(vmem_limit_bytes=24 * MIB),
        name="absorb",
    )(counts, rows, near_field, held, receive)


def in_hbm(array):
    return pltpu.with_memory_space_constraint(array, pltpu.HBM)


def swap(rows, positions):
    channels = rows.shape[-1]
    shaped = rows.reshape(-1, positions, channels)
    return lax.all_to_all(shaped, AXES, 0, 0, tiled=True).reshape(-1, channels)


def body(
    currents, counts, near_source, near_blocks, aggregate, receive, translations, source_blocks
):
    slots = currents.shape[0]
    positions = slots // aggregate.shape[0]
    device = lax.axis_index(AXES)
    local = near_source - (device - 1) * slots
    mirrored = local + 2 * slots - 2 * slots * (local // slots)
    local = jnp.where(device % 2 == 1, mirrored, local)
    count = lax.axis_size("near")
    inner = [(i, i + 1) for i in range(1, count - 1, 2)]
    outer = [(i, i + 1) for i in range(0, count, 2)]
    across = lax.ppermute(currents, "near", inner + [(j, i) for i, j in inner])
    partner = lax.ppermute(currents, "near", outer + [(j, i) for i, j in outer])

    patterns = radiate(in_hbm(counts), in_hbm(currents), in_hbm(aggregate))
    gathered = swap(patterns, positions)
    incoming = translate(in_hbm(source_blocks), gathered, translations, positions)
    returned = swap(incoming, positions)

    local, _ = lax.optimization_barrier((local, incoming))
    near_field, held = near(
        local, across, in_hbm(currents), partner, in_hbm(near_blocks), in_hbm(receive)
    )
    return absorb(in_hbm(counts), returned, held, in_hbm(receive), near_field)


def solution(mesh):
    spread = P(AXES, None, None)
    return jax.shard_map(
        body,
        mesh=mesh,
        in_specs=(
            spread,
            P(),
            P(AXES, None),
            P(AXES, None, None, None),
            P(),
            P(),
            P(None, None, AXES, None, None),
            P(),
        ),
        out_specs=spread,
        check_vma=False,
    )
```

```python
import numpy as np
import jax
import jax.numpy as jnp
from jax import lax
from jax.experimental import pallas as pl
from jax.experimental.pallas import tpu as pltpu
from jax.sharding import PartitionSpec as P

AXES = ("dir", "near")
MIB = 1 << 20
SPLITS = (4, 4)
TILE = 288
SHARES = (2, 2, 4)
HELD = 2


def quarter(v):
    lane = lax.broadcasted_iota(jnp.int32, (1, v.shape[-1]), 1)
    sign = jnp.where(lane < v.shape[-1] // 2, -1.0, 1.0).astype(v.dtype)
    return pltpu.roll(v, v.shape[-1] // 2, 1) * sign


def own_range(counts_ref):
    device = lax.axis_index("dir") * lax.axis_size("near") + lax.axis_index("near")
    odd = device % 2
    return odd * counts_ref[device - odd], counts_ref[device]


def radiate_kernel(
    counts_hbm, currents_hbm, aggregate_hbm, out_hbm, counts_ref, currents_ref, aggregate_ref,
    stacked_ref, sums_ref, rows_ref, out_ref, sems, store_sems,
):
    children, directions, width = aggregate_ref.shape
    unknowns = width // 2
    positions = stacked_ref.shape[1] // 128
    shares = [slice(sum(SPLITS[:i]), sum(SPLITS[: i + 1])) for i in range(len(SPLITS))]
    table = pltpu.make_async_copy(counts_hbm, counts_ref, sems.at[len(shares) + 1])
    table.start()
    own = pltpu.make_async_copy(currents_hbm, currents_ref, sems.at[len(shares)])
    own.start()
    parts = []
    for i, share in enumerate(shares):
        part = pltpu.make_async_copy(
            aggregate_hbm.at[share], aggregate_ref.at[share], sems.at[i]
        )
        part.start()
        parts.append(part)
    table.wait()
    offset, count = own_range(counts_ref)
    own.wait()
    for p in range(positions):
        slot = p - offset
        live = jnp.logical_and(slot >= 0, slot < count)
        row = jnp.clip(slot, 0, positions - 1) * children
        lanes = slice(p * 128, (p + 1) * 128)

        @pl.when(live)
        def _():
            for c in range(children):
                v = currents_ref[row + c]
                stacked_ref[c * width : c * width + unknowns, lanes] = v
                stacked_ref[c * width + unknowns : (c + 1) * width, lanes] = quarter(v)

        @pl.when(jnp.logical_not(live))
        def _():
            stacked_ref[:, lanes] = jnp.zeros((children * width, 128), jnp.bfloat16)

    stores = []
    for i, share in enumerate(shares):
        parts[i].wait()
        for t in range(directions // TILE):
            rows = slice(t * TILE, (t + 1) * TILE)
            total = jnp.dot(
                jnp.concatenate(
                    [aggregate_ref[c, rows, :] for c in range(share.start, share.stop)], axis=1
                ),
                stacked_ref[share.start * width : share.stop * width, :],
                preferred_element_type=jnp.float32,
            )
            if i:
                total += sums_ref[rows, :]
            if i + 1 < len(shares):
                sums_ref[rows, :] = total
                continue
            for p in range(positions):
                rows_ref[pl.ds(p, TILE, stride=positions), :] = total[:, p * 128 : (p + 1) * 128]
            span = slice(t * TILE * positions, (t + 1) * TILE * positions)
            out_ref[span, :] = rows_ref[...].astype(jnp.bfloat16)
            store = pltpu.make_async_copy(out_ref.at[span], out_hbm.at[span], store_sems.at[t])
            store.start()
            stores.append(store)
    for store in stores:
        store.wait()


def radiate(counts, currents, aggregate):
    children, directions, width = aggregate.shape
    positions = currents.shape[0] // children
    tiles = directions // TILE
    hbm = pl.BlockSpec(memory_space=pltpu.HBM)
    return pl.pallas_call(
        radiate_kernel,
        in_specs=[hbm, hbm, hbm],
        out_specs=hbm,
        scratch_shapes=[
            pltpu.SMEM(counts.shape, counts.dtype),
            pltpu.VMEM(currents.shape, currents.dtype),
            pltpu.VMEM(aggregate.shape, aggregate.dtype),
            pltpu.VMEM((children * width, positions * 128), jnp.bfloat16),
            pltpu.VMEM((directions, positions * 128), jnp.float32),
            pltpu.VMEM((TILE * positions, 128), jnp.float32),
            pltpu.VMEM((directions * positions, 128), jnp.bfloat16),
            pltpu.SemaphoreType.DMA((len(SPLITS) + 2,)),
            pltpu.SemaphoreType.DMA((tiles,)),
        ],
        out_shape=jax.ShapeDtypeStruct((directions * positions, 128), jnp.bfloat16),
        compiler_params=pltpu.CompilerParams(vmem_limit_bytes=28 * MIB),
        name="radiate",
    )(counts, currents, aggregate)


def pair_rows(per_group, positions):
    pairs = 4
    select = np.zeros((per_group * pairs * positions, 2 * pairs * per_group * positions))
    for r in range(per_group):
        for pair in range(pairs):
            for p in range(positions):
                row = (r * pairs + pair) * positions + p
                for side in range(2):
                    select[row, ((2 * pair + side) * per_group + r) * positions + p] = 1.0
    return select


def translate_kernel(
    blocks_hbm, rows_ref, translations_ref, select_ref, spread_ref, out_hbm, blocks_ref, values_ref,
    sums_ref, out_ref, sems,
):
    table = pltpu.make_async_copy(blocks_hbm, blocks_ref, sems.at[0])
    table.start()
    block_count, list_length, per_group = translations_ref.shape[:3]
    block = translations_ref.shape[3]
    chunk = select_ref.shape[1]
    groups = rows_ref.shape[0] // chunk
    per_block = groups // block_count
    step = block // per_block
    for h in range(0, groups, 2):
        both = jnp.dot(
            select_ref[...],
            jnp.concatenate(
                [rows_ref[g * chunk : (g + 1) * chunk, :] for g in (h, h + 1)], axis=1
            ),
            preferred_element_type=jnp.float32,
        ).astype(jnp.bfloat16)
        for g in (h, h + 1):
            picked = both[:, (g - h) * 128 : (g - h + 1) * 128]
            other = quarter(picked)
            b = g // per_block
            start = (g % per_block) * step
            for r in range(per_group):
                part = slice(r * step, (r + 1) * step)
                values_ref[b, r, start : start + step, :] = picked[part]
                values_ref[b, r, block + start : block + start + step, :] = other[part]
    table.wait()
    stores = []
    for t in range(block_count):
        sources = [blocks_ref[t, e] for e in range(list_length)]
        for r in range(per_group):
            total = jnp.dot(
                jnp.concatenate([translations_ref[t, e, r] for e in range(list_length)], axis=1),
                jnp.concatenate([values_ref[source, r] for source in sources], axis=0),
                preferred_element_type=jnp.float32,
            )
            total = total.astype(jnp.bfloat16)
            for q in range(per_block):
                sums_ref[t * per_block + q, r * step : (r + 1) * step, :] = total[
                    q * step : (q + 1) * step
                ]
        for h in range(t * per_block, (t + 1) * per_block, 2):
            both = jnp.dot(
                spread_ref[...],
                jnp.concatenate([sums_ref[h], sums_ref[h + 1]], axis=1),
                preferred_element_type=jnp.float32,
            ).astype(jnp.bfloat16)
            for g in (h, h + 1):
                out_ref[g * chunk : (g + 1) * chunk, :] = both[:, (g - h) * 128 : (g - h + 1) * 128]
        span = slice(t * per_block * chunk, (t + 1) * per_block * chunk)
        store = pltpu.make_async_copy(out_ref.at[span], out_hbm.at[span], sems.at[t + 1])
        store.start()
        stores.append(store)
    for store in stores:
        store.wait()


def translate(source_blocks, rows, translations, positions):
    block_count, _, per_group, block, doubled = translations.shape
    select = pair_rows(per_group, positions)
    groups = rows.shape[0] // select.shape[1]
    vmem = pl.BlockSpec(memory_space=pltpu.VMEM)
    return pl.pallas_call(
        translate_kernel,
        in_specs=[pl.BlockSpec(memory_space=pltpu.HBM), vmem, vmem, vmem, vmem],
        out_specs=pl.BlockSpec(memory_space=pltpu.HBM),
        scratch_shapes=[
            pltpu.SMEM(source_blocks.shape, source_blocks.dtype),
            pltpu.VMEM((block_count, per_group, doubled, 128), jnp.bfloat16),
            pltpu.VMEM((groups, select.shape[0], 128), jnp.bfloat16),
            pltpu.VMEM(rows.shape, jnp.bfloat16),
            pltpu.SemaphoreType.DMA((block_count + 1,)),
        ],
        out_shape=jax.ShapeDtypeStruct(rows.shape, jnp.bfloat16),
        compiler_params=pltpu.CompilerParams(vmem_limit_bytes=16 * MIB),
        name="translate",
    )(
        source_blocks,
        rows,
        translations,
        jnp.asarray(select, jnp.bfloat16),
        jnp.asarray(select.T, jnp.bfloat16),
    )


def near_kernel(
    source_ref, across_ref, own_ref, partner_ref, blocks_ref, receive_hbm, out_ref, held_ref,
    window_ref, sem,
):
    slots = own_ref.shape[0]
    unknowns = own_ref.shape[1]
    leaves, terms = blocks_ref.shape[:2]
    first = pl.program_id(0) * leaves
    hold = pltpu.make_async_copy(receive_hbm.at[0:HELD], held_ref, sem)

    @pl.when(first == 0)
    def _():
        hold.start()
        for part, ref in enumerate((across_ref, own_ref, partner_ref)):

            def fill(i, carry, part=part, ref=ref):
                for j in range(4):
                    v = ref[i * 4 + j]
                    row = part * slots + i * 4 + j
                    window_ref[row, 0:unknowns, :] = v
                    window_ref[row, unknowns : 2 * unknowns, :] = quarter(v)
                return carry

            lax.fori_loop(0, slots // 4, fill, 0)

    for i in range(leaves):
        sources = [source_ref[(first + i) * terms + e] for e in range(terms)]
        out_ref[i] = jnp.dot(
            jnp.concatenate([blocks_ref[i, e] for e in range(terms)], axis=1),
            jnp.concatenate([window_ref[source] for source in sources], axis=0),
            preferred_element_type=jnp.float32,
        ).astype(jnp.bfloat16)

    @pl.when(first == slots - leaves)
    def _():
        hold.wait()


def near(source, across, own, partner, blocks, receive):
    slots, unknowns, channels = own.shape
    _, terms, _, doubled = blocks.shape
    leaves = 4
    whole = pl.BlockSpec(own.shape, lambda i, _: (0, 0, 0))
    return pl.pallas_call(
        near_kernel,
        grid_spec=pltpu.PrefetchScalarGridSpec(
            num_scalar_prefetch=1,
            grid=(slots // leaves,),
            in_specs=[
                whole,
                whole,
                whole,
                pl.BlockSpec((leaves, terms, unknowns, doubled), lambda i, _: (i, 0, 0, 0)),
                pl.BlockSpec(memory_space=pltpu.HBM),
            ],
            out_specs=[
                pl.BlockSpec((leaves, unknowns, channels), lambda i, _: (i, 0, 0)),
                pl.BlockSpec(memory_space=pl.ANY),
            ],
            scratch_shapes=[
                pltpu.VMEM((3 * slots, doubled, channels), jnp.bfloat16),
                pltpu.SemaphoreType.DMA,
            ],
        ),
        out_shape=[
            jax.ShapeDtypeStruct((slots, unknowns, channels), jnp.bfloat16),
            jax.ShapeDtypeStruct((HELD,) + receive.shape[1:], receive.dtype),
        ],
        compiler_params=pltpu.CompilerParams(vmem_limit_bytes=28 * MIB),
        cost_estimate=pl.CostEstimate(flops=10**10, transcendentals=0, bytes_accessed=2 * 10**7),
        name="near",
    )(source.reshape(-1), across, own, partner, blocks, receive)


def absorb_kernel(
    counts_hbm, rows_ref, near_ref, held_ref, receive_hbm, out_hbm, counts_ref, wide_ref,
    doubled_ref, receive_ref, fields_ref, fetch_sems, store_sems,
):
    children, unknowns, doubled = receive_hbm.shape
    directions = doubled // 2
    positions = doubled_ref.shape[1] // 128
    spans = [slice(sum(SHARES[:q]), sum(SHARES[: q + 1])) for q in range(len(SHARES))]
    table = pltpu.make_async_copy(counts_hbm, counts_ref, fetch_sems.at[0])
    table.start()
    parts = [None]
    for q in range(1, len(SHARES)):
        span = slice(spans[q].start - HELD, spans[q].stop - HELD)
        part = pltpu.make_async_copy(
            receive_hbm.at[spans[q]], receive_ref.at[span], fetch_sems.at[q]
        )
        part.start()
        parts.append(part)
    wide_ref[...] = rows_ref[...].astype(jnp.float32)
    for p in range(positions):
        v = wide_ref[pl.ds(p, directions, stride=positions), :].astype(jnp.bfloat16)
        doubled_ref[0:directions, p * 128 : (p + 1) * 128] = v
        doubled_ref[directions:doubled, p * 128 : (p + 1) * 128] = quarter(v)
    table.wait()
    offset, count = own_range(counts_ref)
    for slot in range(positions):

        @pl.when(slot >= count)
        def _():
            fields_ref[slot * children : (slot + 1) * children] = jnp.zeros(
                (children, unknowns, 128), jnp.bfloat16
            )

    stores = []
    for q, octants in enumerate(SHARES):
        base = spans[q].start
        if q:
            parts[q].wait()
        held = receive_ref[base - HELD : base - HELD + octants] if q else held_ref[...]
        lines = held.reshape(octants * unknowns, doubled)
        far = jnp.dot(lines, doubled_ref[...], preferred_element_type=jnp.float32)
        for p in range(positions):
            slot = p - offset

            @pl.when(jnp.logical_and(slot >= 0, slot < count))
            def _():
                for c in range(octants):
                    leaf = slot * children + base + c
                    part = far[c * unknowns : (c + 1) * unknowns, p * 128 : (p + 1) * 128]
                    fields_ref[leaf] = (part + near_ref[leaf]).astype(jnp.bfloat16)

        for slot in range(positions):
            span = pl.ds(slot * children + base, octants)
            store = pltpu.make_async_copy(
                fields_ref.at[span], out_hbm.at[span], store_sems.at[q, slot]
            )
            store.start()
            stores.append(store)
    for store in stores:
        store.wait()


def absorb(counts, rows, held, receive, near_field):
    children, _, doubled = receive.shape
    positions = near_field.shape[0] // children
    steps = len(SHARES)
    vmem = pl.BlockSpec(memory_space=pltpu.VMEM)
    hbm = pl.BlockSpec(memory_space=pltpu.HBM)
    return pl.pallas_call(
        absorb_kernel,
        in_specs=[hbm, vmem, vmem, vmem, hbm],
        out_specs=hbm,
        scratch_shapes=[
            pltpu.SMEM(counts.shape, counts.dtype),
            pltpu.VMEM(rows.shape, jnp.float32),
            pltpu.VMEM((doubled, positions * 128), jnp.bfloat16),
            pltpu.VMEM((children - HELD,) + receive.shape[1:], receive.dtype),
            pltpu.VMEM(near_field.shape, jnp.bfloat16),
            pltpu.SemaphoreType.DMA((steps,)),
            pltpu.SemaphoreType.DMA((steps, positions)),
        ],
        out_shape=jax.ShapeDtypeStruct(near_field.shape, jnp.bfloat16),
        compiler_params=pltpu.CompilerParams(vmem_limit_bytes=24 * MIB),
        name="absorb",
    )(counts, rows, near_field, held, receive)


def in_hbm(array):
    return pltpu.with_memory_space_constraint(array, pltpu.HBM)


def swap(rows, positions):
    channels = rows.shape[-1]
    shaped = rows.reshape(-1, positions, channels)
    return lax.all_to_all(shaped, AXES, 0, 0, tiled=True).reshape(-1, channels)


def body(
    currents, counts, near_source, near_blocks, aggregate, receive, translations, source_blocks
):
    slots = currents.shape[0]
    positions = slots // aggregate.shape[0]
    device = lax.axis_index(AXES)
    local = near_source - (device - 1) * slots
    mirrored = local + 2 * slots - 2 * slots * (local // slots)
    local = jnp.where(device % 2 == 1, mirrored, local)
    count = lax.axis_size("near")
    inner = [(i, i + 1) for i in range(1, count - 1, 2)]
    outer = [(i, i + 1) for i in range(0, count, 2)]
    across = lax.ppermute(currents, "near", inner + [(j, i) for i, j in inner])
    partner = lax.ppermute(currents, "near", outer + [(j, i) for i, j in outer])

    patterns = radiate(in_hbm(counts), in_hbm(currents), in_hbm(aggregate))
    gathered = swap(patterns, positions)
    incoming = translate(in_hbm(source_blocks), gathered, translations, positions)
    returned = swap(incoming, positions)

    local, _ = lax.optimization_barrier((local, incoming))
    near_field, held = near(
        local, across, in_hbm(currents), partner, in_hbm(near_blocks), in_hbm(receive)
    )
    return absorb(in_hbm(counts), returned, held, in_hbm(receive), near_field)


def solution(mesh):
    spread = P(AXES, None, None)
    return jax.shard_map(
        body,
        mesh=mesh,
        in_specs=(
            spread,
            P(),
            P(AXES, None),
            P(AXES, None, None, None),
            P(),
            P(),
            P(None, None, AXES, None, None),
            P(),
        ),
        out_specs=spread,
        check_vma=False,
    )
```

```python
import numpy as np
import jax
import jax.numpy as jnp
from jax import lax
from jax.experimental import pallas as pl
from jax.experimental.pallas import tpu as pltpu
from jax.sharding import PartitionSpec as P

AXES = ("dir", "near")
MIB = 1 << 20
SPLITS = (4, 4)
TILE = 288
SHARES = (2, 2, 4)
HELD = 2


def quarter(v):
    lane = lax.broadcasted_iota(jnp.int32, (1, v.shape[-1]), 1)
    sign = jnp.where(lane < v.shape[-1] // 2, -1.0, 1.0).astype(v.dtype)
    return pltpu.roll(v, v.shape[-1] // 2, 1) * sign


def own_range(counts_ref):
    device = lax.axis_index("dir") * lax.axis_size("near") + lax.axis_index("near")
    odd = device % 2
    return odd * counts_ref[device - odd], counts_ref[device]


def radiate_kernel(
    counts_hbm, currents_hbm, aggregate_hbm, out_hbm, counts_ref, currents_ref, aggregate_ref,
    stacked_ref, sums_ref, rows_ref, out_ref, sems, store_sems,
):
    children, directions, width = aggregate_ref.shape
    unknowns = width // 2
    positions = stacked_ref.shape[1] // 128
    shares = [slice(sum(SPLITS[:i]), sum(SPLITS[: i + 1])) for i in range(len(SPLITS))]
    table = pltpu.make_async_copy(counts_hbm, counts_ref, sems.at[len(shares) + 1])
    table.start()
    own = pltpu.make_async_copy(currents_hbm, currents_ref, sems.at[len(shares)])
    own.start()
    parts = []
    for i, share in enumerate(shares):
        part = pltpu.make_async_copy(
            aggregate_hbm.at[share], aggregate_ref.at[share], sems.at[i]
        )
        part.start()
        parts.append(part)
    table.wait()
    offset, count = own_range(counts_ref)
    own.wait()
    for p in range(positions):
        slot = p - offset
        live = jnp.logical_and(slot >= 0, slot < count)
        row = jnp.clip(slot, 0, positions - 1) * children
        lanes = slice(p * 128, (p + 1) * 128)

        @pl.when(live)
        def _():
            for c in range(children):
                v = currents_ref[row + c]
                stacked_ref[c * width : c * width + unknowns, lanes] = v
                stacked_ref[c * width + unknowns : (c + 1) * width, lanes] = quarter(v)

        @pl.when(jnp.logical_not(live))
        def _():
            stacked_ref[:, lanes] = jnp.zeros((children * width, 128), jnp.bfloat16)

    stores = []
    for i, share in enumerate(shares):
        parts[i].wait()
        for t in range(directions // TILE):
            rows = slice(t * TILE, (t + 1) * TILE)
            total = jnp.dot(
                jnp.concatenate(
                    [aggregate_ref[c, rows, :] for c in range(share.start, share.stop)], axis=1
                ),
                stacked_ref[share.start * width : share.stop * width, :],
                preferred_element_type=jnp.float32,
            )
            if i:
                total += sums_ref[rows, :]
            if i + 1 < len(shares):
                sums_ref[rows, :] = total
                continue
            for p in range(positions):
                rows_ref[pl.ds(p, TILE, stride=positions), :] = total[:, p * 128 : (p + 1) * 128]
            span = slice(t * TILE * positions, (t + 1) * TILE * positions)
            out_ref[span, :] = rows_ref[...].astype(jnp.bfloat16)
            store = pltpu.make_async_copy(out_ref.at[span], out_hbm.at[span], store_sems.at[t])
            store.start()
            stores.append(store)
    for store in stores:
        store.wait()


def radiate(counts, currents, aggregate):
    children, directions, width = aggregate.shape
    positions = currents.shape[0] // children
    tiles = directions // TILE
    hbm = pl.BlockSpec(memory_space=pltpu.HBM)
    return pl.pallas_call(
        radiate_kernel,
        in_specs=[hbm, hbm, hbm],
        out_specs=hbm,
        scratch_shapes=[
            pltpu.SMEM(counts.shape, counts.dtype),
            pltpu.VMEM(currents.shape, currents.dtype),
            pltpu.VMEM(aggregate.shape, aggregate.dtype),
            pltpu.VMEM((children * width, positions * 128), jnp.bfloat16),
            pltpu.VMEM((directions, positions * 128), jnp.float32),
            pltpu.VMEM((TILE * positions, 128), jnp.float32),
            pltpu.VMEM((directions * positions, 128), jnp.bfloat16),
            pltpu.SemaphoreType.DMA((len(SPLITS) + 2,)),
            pltpu.SemaphoreType.DMA((tiles,)),
        ],
        out_shape=jax.ShapeDtypeStruct((directions * positions, 128), jnp.bfloat16),
        compiler_params=pltpu.CompilerParams(vmem_limit_bytes=28 * MIB),
        name="radiate",
    )(counts, currents, aggregate)


def pair_rows(per_group, positions):
    pairs = 4
    select = np.zeros((per_group * pairs * positions, 2 * pairs * per_group * positions))
    for r in range(per_group):
        for pair in range(pairs):
            for p in range(positions):
                row = (r * pairs + pair) * positions + p
                for side in range(2):
                    select[row, ((2 * pair + side) * per_group + r) * positions + p] = 1.0
    return select


def translate_kernel(
    blocks_hbm, rows_ref, translations_ref, select_ref, spread_ref, out_hbm, blocks_ref, values_ref,
    sums_ref, out_ref, sems,
):
    table = pltpu.make_async_copy(blocks_hbm, blocks_ref, sems.at[0])
    table.start()
    block_count, list_length, per_group = translations_ref.shape[:3]
    block = translations_ref.shape[3]
    chunk = select_ref.shape[1]
    groups = rows_ref.shape[0] // chunk
    per_block = groups // block_count
    step = block // per_block
    for h in range(0, groups, 2):
        both = jnp.dot(
            select_ref[...],
            jnp.concatenate(
                [rows_ref[g * chunk : (g + 1) * chunk, :] for g in (h, h + 1)], axis=1
            ),
            preferred_element_type=jnp.float32,
        ).astype(jnp.bfloat16)
        for g in (h, h + 1):
            picked = both[:, (g - h) * 128 : (g - h + 1) * 128]
            other = quarter(picked)
            b = g // per_block
            start = (g % per_block) * step
            for r in range(per_group):
                part = slice(r * step, (r + 1) * step)
                values_ref[b, r, start : start + step, :] = picked[part]
                values_ref[b, r, block + start : block + start + step, :] = other[part]
    table.wait()
    stores = []
    for t in range(block_count):
        sources = [blocks_ref[t, e] for e in range(list_length)]
        for r in range(per_group):
            total = jnp.dot(
                jnp.concatenate([translations_ref[t, e, r] for e in range(list_length)], axis=1),
                jnp.concatenate([values_ref[source, r] for source in sources], axis=0),
                preferred_element_type=jnp.float32,
            )
            total = total.astype(jnp.bfloat16)
            for q in range(per_block):
                sums_ref[t * per_block + q, r * step : (r + 1) * step, :] = total[
                    q * step : (q + 1) * step
                ]
        for h in range(t * per_block, (t + 1) * per_block, 2):
            both = jnp.dot(
                spread_ref[...],
                jnp.concatenate([sums_ref[h], sums_ref[h + 1]], axis=1),
                preferred_element_type=jnp.float32,
            ).astype(jnp.bfloat16)
            for g in (h, h + 1):
                out_ref[g * chunk : (g + 1) * chunk, :] = both[:, (g - h) * 128 : (g - h + 1) * 128]
        span = slice(t * per_block * chunk, (t + 1) * per_block * chunk)
        store = pltpu.make_async_copy(out_ref.at[span], out_hbm.at[span], sems.at[t + 1])
        store.start()
        stores.append(store)
    for store in stores:
        store.wait()


def translate(source_blocks, rows, translations, positions):
    block_count, _, per_group, block, doubled = translations.shape
    select = pair_rows(per_group, positions)
    groups = rows.shape[0] // select.shape[1]
    vmem = pl.BlockSpec(memory_space=pltpu.VMEM)
    return pl.pallas_call(
        translate_kernel,
        in_specs=[pl.BlockSpec(memory_space=pltpu.HBM), vmem, vmem, vmem, vmem],
        out_specs=pl.BlockSpec(memory_space=pltpu.HBM),
        scratch_shapes=[
            pltpu.SMEM(source_blocks.shape, source_blocks.dtype),
            pltpu.VMEM((block_count, per_group, doubled, 128), jnp.bfloat16),
            pltpu.VMEM((groups, select.shape[0], 128), jnp.bfloat16),
            pltpu.VMEM(rows.shape, jnp.bfloat16),
            pltpu.SemaphoreType.DMA((block_count + 1,)),
        ],
        out_shape=jax.ShapeDtypeStruct(rows.shape, jnp.bfloat16),
        compiler_params=pltpu.CompilerParams(vmem_limit_bytes=16 * MIB),
        name="translate",
    )(
        source_blocks,
        rows,
        translations,
        jnp.asarray(select, jnp.bfloat16),
        jnp.asarray(select.T, jnp.bfloat16),
    )


def near_kernel(
    source_ref, across_ref, own_ref, partner_ref, blocks_ref, receive_hbm, out_ref, held_ref,
    window_ref, sem,
):
    slots = own_ref.shape[0]
    unknowns = own_ref.shape[1]
    leaves, terms = blocks_ref.shape[:2]
    first = pl.program_id(0) * leaves
    hold = pltpu.make_async_copy(receive_hbm.at[0:HELD], held_ref, sem)

    @pl.when(first == 0)
    def _():
        hold.start()
        for part, ref in enumerate((across_ref, own_ref, partner_ref)):

            def fill(i, carry, part=part, ref=ref):
                for j in range(4):
                    v = ref[i * 4 + j]
                    row = part * slots + i * 4 + j
                    window_ref[row, 0:unknowns, :] = v
                    window_ref[row, unknowns : 2 * unknowns, :] = quarter(v)
                return carry

            lax.fori_loop(0, slots // 4, fill, 0)

    for i in range(leaves):
        sources = [source_ref[(first + i) * terms + e] for e in range(terms)]
        out_ref[i] = jnp.dot(
            jnp.concatenate([blocks_ref[i, e] for e in range(terms)], axis=1),
            jnp.concatenate([window_ref[source] for source in sources], axis=0),
            preferred_element_type=jnp.float32,
        ).astype(jnp.bfloat16)

    @pl.when(first == slots - leaves)
    def _():
        hold.wait()


def near(source, across, own, partner, blocks, receive):
    slots, unknowns, channels = own.shape
    _, terms, _, doubled = blocks.shape
    leaves = 4
    whole = pl.BlockSpec(own.shape, lambda i, _: (0, 0, 0))
    return pl.pallas_call(
        near_kernel,
        grid_spec=pltpu.PrefetchScalarGridSpec(
            num_scalar_prefetch=1,
            grid=(slots // leaves,),
            in_specs=[
                whole,
                whole,
                whole,
                pl.BlockSpec((leaves, terms, unknowns, doubled), lambda i, _: (i, 0, 0, 0)),
                pl.BlockSpec(memory_space=pltpu.HBM),
            ],
            out_specs=[
                pl.BlockSpec((leaves, unknowns, channels), lambda i, _: (i, 0, 0)),
                pl.BlockSpec(memory_space=pl.ANY),
            ],
            scratch_shapes=[
                pltpu.VMEM((3 * slots, doubled, channels), jnp.bfloat16),
                pltpu.SemaphoreType.DMA,
            ],
        ),
        out_shape=[
            jax.ShapeDtypeStruct((slots, unknowns, channels), jnp.bfloat16),
            jax.ShapeDtypeStruct((HELD,) + receive.shape[1:], receive.dtype),
        ],
        compiler_params=pltpu.CompilerParams(vmem_limit_bytes=28 * MIB),
        cost_estimate=pl.CostEstimate(flops=10**10, transcendentals=0, bytes_accessed=2 * 10**7),
        name="near",
    )(source.reshape(-1), across, own, partner, blocks, receive)


def absorb_kernel(
    counts_hbm, rows_ref, near_ref, held_ref, receive_hbm, out_hbm, counts_ref, wide_ref,
    doubled_ref, receive_ref, fields_ref, fetch_sems, store_sems,
):
    children, unknowns, doubled = receive_hbm.shape
    directions = doubled // 2
    positions = doubled_ref.shape[1] // 128
    spans = [slice(sum(SHARES[:q]), sum(SHARES[: q + 1])) for q in range(len(SHARES))]
    table = pltpu.make_async_copy(counts_hbm, counts_ref, fetch_sems.at[0])
    table.start()
    parts = [None]
    for q in range(1, len(SHARES)):
        span = slice(spans[q].start - HELD, spans[q].stop - HELD)
        part = pltpu.make_async_copy(
            receive_hbm.at[spans[q]], receive_ref.at[span], fetch_sems.at[q]
        )
        part.start()
        parts.append(part)
    wide_ref[...] = rows_ref[...].astype(jnp.float32)
    for p in range(positions):
        v = wide_ref[pl.ds(p, directions, stride=positions), :].astype(jnp.bfloat16)
        doubled_ref[0:directions, p * 128 : (p + 1) * 128] = v
        doubled_ref[directions:doubled, p * 128 : (p + 1) * 128] = quarter(v)
    table.wait()
    offset, count = own_range(counts_ref)
    for slot in range(positions):

        @pl.when(slot >= count)
        def _():
            fields_ref[slot * children : (slot + 1) * children] = jnp.zeros(
                (children, unknowns, 128), jnp.bfloat16
            )

    stores = []
    for q, octants in enumerate(SHARES):
        base = spans[q].start
        if q:
            parts[q].wait()
        held = receive_ref[base - HELD : base - HELD + octants] if q else held_ref[...]
        lines = held.reshape(octants * unknowns, doubled)
        far = jnp.dot(lines, doubled_ref[...], preferred_element_type=jnp.float32)
        for p in range(positions):
            slot = p - offset

            @pl.when(jnp.logical_and(slot >= 0, slot < count))
            def _():
                for c in range(octants):
                    leaf = slot * children + base + c
                    part = far[c * unknowns : (c + 1) * unknowns, p * 128 : (p + 1) * 128]
                    fields_ref[leaf] = (part + near_ref[leaf]).astype(jnp.bfloat16)

        for slot in range(positions):
            span = pl.ds(slot * children + base, octants)
            store = pltpu.make_async_copy(
                fields_ref.at[span], out_hbm.at[span], store_sems.at[q, slot]
            )
            store.start()
            stores.append(store)
    for store in stores:
        store.wait()


def absorb(counts, rows, held, receive, near_field):
    children, _, doubled = receive.shape
    positions = near_field.shape[0] // children
    steps = len(SHARES)
    vmem = pl.BlockSpec(memory_space=pltpu.VMEM)
    hbm = pl.BlockSpec(memory_space=pltpu.HBM)
    return pl.pallas_call(
        absorb_kernel,
        in_specs=[hbm, vmem, vmem, vmem, hbm],
        out_specs=hbm,
        scratch_shapes=[
            pltpu.SMEM(counts.shape, counts.dtype),
            pltpu.VMEM(rows.shape, jnp.float32),
            pltpu.VMEM((doubled, positions * 128), jnp.bfloat16),
            pltpu.VMEM((children - HELD,) + receive.shape[1:], receive.dtype),
            pltpu.VMEM(near_field.shape, jnp.bfloat16),
            pltpu.SemaphoreType.DMA((steps,)),
            pltpu.SemaphoreType.DMA((steps, positions)),
        ],
        out_shape=jax.ShapeDtypeStruct(near_field.shape, jnp.bfloat16),
        compiler_params=pltpu.CompilerParams(vmem_limit_bytes=24 * MIB),
        name="absorb",
    )(counts, rows, near_field, held, receive)


def arrive_kernel(array_ref, out_ref):
    pass


def arrive(array):
    hbm = pl.BlockSpec(memory_space=pltpu.HBM)
    return pl.pallas_call(
        arrive_kernel,
        in_specs=[hbm],
        out_specs=hbm,
        out_shape=jax.ShapeDtypeStruct(array.shape, array.dtype),
        input_output_aliases={0: 0},
        cost_estimate=pl.CostEstimate(flops=5 * 10**10, transcendentals=0, bytes_accessed=10**7),
        name="arrive",
    )(array)


def in_hbm(array):
    return pltpu.with_memory_space_constraint(array, pltpu.HBM)


def swap(rows, positions):
    channels = rows.shape[-1]
    shaped = rows.reshape(-1, positions, channels)
    return lax.all_to_all(shaped, AXES, 0, 0, tiled=True).reshape(-1, channels)


def body(
    currents, counts, near_source, near_blocks, aggregate, receive, translations, source_blocks
):
    slots = currents.shape[0]
    positions = slots // aggregate.shape[0]
    device = lax.axis_index(AXES)
    local = near_source - (device - 1) * slots
    mirrored = local + 2 * slots - 2 * slots * (local // slots)
    local = jnp.where(device % 2 == 1, mirrored, local)
    count = lax.axis_size("near")
    inner = [(i, i + 1) for i in range(1, count - 1, 2)]
    outer = [(i, i + 1) for i in range(0, count, 2)]
    across = lax.ppermute(currents, "near", inner + [(j, i) for i, j in inner])
    partner = lax.ppermute(currents, "near", outer + [(j, i) for i, j in outer])

    patterns = radiate(in_hbm(counts), in_hbm(currents), in_hbm(aggregate))
    gathered = swap(patterns, positions)
    gathered, partner = lax.optimization_barrier((gathered, arrive(partner)))
    incoming = translate(in_hbm(source_blocks), gathered, translations, positions)
    returned = swap(incoming, positions)

    local, _ = lax.optimization_barrier((local, incoming))
    near_field, held = near(
        local, across, in_hbm(currents), partner, in_hbm(near_blocks), in_hbm(receive)
    )
    return absorb(in_hbm(counts), returned, held, in_hbm(receive), near_field)


def solution(mesh):
    spread = P(AXES, None, None)
    return jax.shard_map(
        body,
        mesh=mesh,
        in_specs=(
            spread,
            P(),
            P(AXES, None),
            P(AXES, None, None, None),
            P(),
            P(),
            P(None, None, AXES, None, None),
            P(),
        ),
        out_specs=spread,
        check_vma=False,
    )
```

```python
import numpy as np
import jax
import jax.numpy as jnp
from jax import lax
from jax.experimental import pallas as pl
from jax.experimental.pallas import tpu as pltpu
from jax.sharding import PartitionSpec as P

AXES = ("dir", "near")
MIB = 1 << 20
SPLITS = (4, 4)
TILE = 288
SHARES = (2, 2, 4)
HELD = 2


def quarter(v):
    lane = lax.broadcasted_iota(jnp.int32, (1, v.shape[-1]), 1)
    sign = jnp.where(lane < v.shape[-1] // 2, -1.0, 1.0).astype(v.dtype)
    return pltpu.roll(v, v.shape[-1] // 2, 1) * sign


def own_range(counts_ref):
    device = lax.axis_index("dir") * lax.axis_size("near") + lax.axis_index("near")
    odd = device % 2
    return odd * counts_ref[device - odd], counts_ref[device]


def radiate_kernel(
    counts_hbm, currents_hbm, aggregate_hbm, out_hbm, counts_ref, currents_ref, aggregate_ref,
    stacked_ref, sums_ref, rows_ref, out_ref, sems, store_sems,
):
    children, directions, width = aggregate_ref.shape
    unknowns = width // 2
    positions = stacked_ref.shape[1] // 128
    shares = [slice(sum(SPLITS[:i]), sum(SPLITS[: i + 1])) for i in range(len(SPLITS))]
    table = pltpu.make_async_copy(counts_hbm, counts_ref, sems.at[len(shares) + 1])
    table.start()
    own = pltpu.make_async_copy(currents_hbm, currents_ref, sems.at[len(shares)])
    own.start()
    parts = []
    for i, share in enumerate(shares):
        part = pltpu.make_async_copy(
            aggregate_hbm.at[share], aggregate_ref.at[share], sems.at[i]
        )
        part.start()
        parts.append(part)
    table.wait()
    offset, count = own_range(counts_ref)
    own.wait()
    for p in range(positions):
        slot = p - offset
        live = jnp.logical_and(slot >= 0, slot < count)
        row = jnp.clip(slot, 0, positions - 1) * children
        lanes = slice(p * 128, (p + 1) * 128)

        @pl.when(live)
        def _():
            for c in range(children):
                v = currents_ref[row + c]
                stacked_ref[c * width : c * width + unknowns, lanes] = v
                stacked_ref[c * width + unknowns : (c + 1) * width, lanes] = quarter(v)

        @pl.when(jnp.logical_not(live))
        def _():
            stacked_ref[:, lanes] = jnp.zeros((children * width, 128), jnp.bfloat16)

    stores = []
    for i, share in enumerate(shares):
        parts[i].wait()
        for t in range(directions // TILE):
            rows = slice(t * TILE, (t + 1) * TILE)
            total = jnp.dot(
                jnp.concatenate(
                    [aggregate_ref[c, rows, :] for c in range(share.start, share.stop)], axis=1
                ),
                stacked_ref[share.start * width : share.stop * width, :],
                preferred_element_type=jnp.float32,
            )
            if i:
                total += sums_ref[rows, :]
            if i + 1 < len(shares):
                sums_ref[rows, :] = total
                continue
            for p in range(positions):
                rows_ref[pl.ds(p, TILE, stride=positions), :] = total[:, p * 128 : (p + 1) * 128]
            span = slice(t * TILE * positions, (t + 1) * TILE * positions)
            out_ref[span, :] = rows_ref[...].astype(jnp.bfloat16)
            store = pltpu.make_async_copy(out_ref.at[span], out_hbm.at[span], store_sems.at[t])
            store.start()
            stores.append(store)
    for store in stores:
        store.wait()


def radiate(counts, currents, aggregate):
    children, directions, width = aggregate.shape
    positions = currents.shape[0] // children
    tiles = directions // TILE
    hbm = pl.BlockSpec(memory_space=pltpu.HBM)
    return pl.pallas_call(
        radiate_kernel,
        in_specs=[hbm, hbm, hbm],
        out_specs=hbm,
        scratch_shapes=[
            pltpu.SMEM(counts.shape, counts.dtype),
            pltpu.VMEM(currents.shape, currents.dtype),
            pltpu.VMEM(aggregate.shape, aggregate.dtype),
            pltpu.VMEM((children * width, positions * 128), jnp.bfloat16),
            pltpu.VMEM((directions, positions * 128), jnp.float32),
            pltpu.VMEM((TILE * positions, 128), jnp.float32),
            pltpu.VMEM((directions * positions, 128), jnp.bfloat16),
            pltpu.SemaphoreType.DMA((len(SPLITS) + 2,)),
            pltpu.SemaphoreType.DMA((tiles,)),
        ],
        out_shape=jax.ShapeDtypeStruct((directions * positions, 128), jnp.bfloat16),
        compiler_params=pltpu.CompilerParams(vmem_limit_bytes=28 * MIB),
        name="radiate",
    )(counts, currents, aggregate)


def pair_rows(per_group, positions):
    pairs = 4
    select = np.zeros((per_group * pairs * positions, 2 * pairs * per_group * positions))
    for r in range(per_group):
        for pair in range(pairs):
            for p in range(positions):
                row = (r * pairs + pair) * positions + p
                for side in range(2):
                    select[row, ((2 * pair + side) * per_group + r) * positions + p] = 1.0
    return select


def translate_kernel(
    blocks_hbm, rows_ref, translations_ref, select_ref, spread_ref, out_hbm, blocks_ref, values_ref,
    sums_ref, out_ref, sems,
):
    table = pltpu.make_async_copy(blocks_hbm, blocks_ref, sems.at[0])
    table.start()
    block_count, list_length, per_group = translations_ref.shape[:3]
    block = translations_ref.shape[3]
    chunk = select_ref.shape[1]
    groups = rows_ref.shape[0] // chunk
    per_block = groups // block_count
    step = block // per_block
    for h in range(0, groups, 2):
        both = jnp.dot(
            select_ref[...],
            jnp.concatenate(
                [rows_ref[g * chunk : (g + 1) * chunk, :] for g in (h, h + 1)], axis=1
            ),
            preferred_element_type=jnp.float32,
        ).astype(jnp.bfloat16)
        for g in (h, h + 1):
            picked = both[:, (g - h) * 128 : (g - h + 1) * 128]
            other = quarter(picked)
            b = g // per_block
            start = (g % per_block) * step
            for r in range(per_group):
                part = slice(r * step, (r + 1) * step)
                values_ref[b, r, start : start + step, :] = picked[part]
                values_ref[b, r, block + start : block + start + step, :] = other[part]
    table.wait()
    stores = []
    for t in range(block_count):
        sources = [blocks_ref[t, e] for e in range(list_length)]
        for r in range(per_group):
            total = jnp.dot(
                jnp.concatenate([translations_ref[t, e, r] for e in range(list_length)], axis=1),
                jnp.concatenate([values_ref[source, r] for source in sources], axis=0),
                preferred_element_type=jnp.float32,
            )
            total = total.astype(jnp.bfloat16)
            for q in range(per_block):
                sums_ref[t * per_block + q, r * step : (r + 1) * step, :] = total[
                    q * step : (q + 1) * step
                ]
        for h in range(t * per_block, (t + 1) * per_block, 2):
            both = jnp.dot(
                spread_ref[...],
                jnp.concatenate([sums_ref[h], sums_ref[h + 1]], axis=1),
                preferred_element_type=jnp.float32,
            ).astype(jnp.bfloat16)
            for g in (h, h + 1):
                out_ref[g * chunk : (g + 1) * chunk, :] = both[:, (g - h) * 128 : (g - h + 1) * 128]
        span = slice(t * per_block * chunk, (t + 1) * per_block * chunk)
        store = pltpu.make_async_copy(out_ref.at[span], out_hbm.at[span], sems.at[t + 1])
        store.start()
        stores.append(store)
    for store in stores:
        store.wait()


def translate(source_blocks, rows, translations, positions):
    block_count, _, per_group, block, doubled = translations.shape
    select = pair_rows(per_group, positions)
    groups = rows.shape[0] // select.shape[1]
    vmem = pl.BlockSpec(memory_space=pltpu.VMEM)
    return pl.pallas_call(
        translate_kernel,
        in_specs=[pl.BlockSpec(memory_space=pltpu.HBM), vmem, vmem, vmem, vmem],
        out_specs=pl.BlockSpec(memory_space=pltpu.HBM),
        scratch_shapes=[
            pltpu.SMEM(source_blocks.shape, source_blocks.dtype),
            pltpu.VMEM((block_count, per_group, doubled, 128), jnp.bfloat16),
            pltpu.VMEM((groups, select.shape[0], 128), jnp.bfloat16),
            pltpu.VMEM(rows.shape, jnp.bfloat16),
            pltpu.SemaphoreType.DMA((block_count + 1,)),
        ],
        out_shape=jax.ShapeDtypeStruct(rows.shape, jnp.bfloat16),
        compiler_params=pltpu.CompilerParams(vmem_limit_bytes=16 * MIB),
        name="translate",
    )(
        source_blocks,
        rows,
        translations,
        jnp.asarray(select, jnp.bfloat16),
        jnp.asarray(select.T, jnp.bfloat16),
    )


def near_kernel(
    source_ref, across_ref, own_ref, partner_ref, blocks_ref, receive_hbm, out_ref, held_ref,
    window_ref, sem,
):
    slots = own_ref.shape[0]
    unknowns = own_ref.shape[1]
    leaves, terms = blocks_ref.shape[:2]
    first = pl.program_id(0) * leaves
    hold = pltpu.make_async_copy(receive_hbm.at[0:HELD], held_ref, sem)

    @pl.when(first == 0)
    def _():
        hold.start()
        for part, ref in enumerate((across_ref, own_ref, partner_ref)):

            def fill(i, carry, part=part, ref=ref):
                for j in range(4):
                    v = ref[i * 4 + j]
                    row = part * slots + i * 4 + j
                    window_ref[row, 0:unknowns, :] = v
                    window_ref[row, unknowns : 2 * unknowns, :] = quarter(v)
                return carry

            lax.fori_loop(0, slots // 4, fill, 0)

    for i in range(leaves):
        sources = [source_ref[(first + i) * terms + e] for e in range(terms)]
        out_ref[i] = jnp.dot(
            jnp.concatenate([blocks_ref[i, e] for e in range(terms)], axis=1),
            jnp.concatenate([window_ref[source] for source in sources], axis=0),
            preferred_element_type=jnp.float32,
        ).astype(jnp.bfloat16)

    @pl.when(first == slots - leaves)
    def _():
        hold.wait()


def near(source, across, own, partner, blocks, receive):
    slots, unknowns, channels = own.shape
    _, terms, _, doubled = blocks.shape
    leaves = 8
    whole = pl.BlockSpec(own.shape, lambda i, _: (0, 0, 0))
    return pl.pallas_call(
        near_kernel,
        grid_spec=pltpu.PrefetchScalarGridSpec(
            num_scalar_prefetch=1,
            grid=(slots // leaves,),
            in_specs=[
                whole,
                whole,
                whole,
                pl.BlockSpec((leaves, terms, unknowns, doubled), lambda i, _: (i, 0, 0, 0)),
                pl.BlockSpec(memory_space=pltpu.HBM),
            ],
            out_specs=[
                pl.BlockSpec((leaves, unknowns, channels), lambda i, _: (i, 0, 0)),
                pl.BlockSpec(memory_space=pl.ANY),
            ],
            scratch_shapes=[
                pltpu.VMEM((3 * slots, doubled, channels), jnp.bfloat16),
                pltpu.SemaphoreType.DMA,
            ],
        ),
        out_shape=[
            jax.ShapeDtypeStruct((slots, unknowns, channels), jnp.bfloat16),
            jax.ShapeDtypeStruct((HELD,) + receive.shape[1:], receive.dtype),
        ],
        compiler_params=pltpu.CompilerParams(vmem_limit_bytes=28 * MIB),
        cost_estimate=pl.CostEstimate(flops=10**10, transcendentals=0, bytes_accessed=2 * 10**7),
        name="near",
    )(source.reshape(-1), across, own, partner, blocks, receive)


def absorb_kernel(
    counts_hbm, rows_ref, near_ref, held_ref, receive_hbm, out_hbm, counts_ref, wide_ref,
    doubled_ref, receive_ref, fields_ref, fetch_sems, store_sems,
):
    children, unknowns, doubled = receive_hbm.shape
    directions = doubled // 2
    positions = doubled_ref.shape[1] // 128
    spans = [slice(sum(SHARES[:q]), sum(SHARES[: q + 1])) for q in range(len(SHARES))]
    table = pltpu.make_async_copy(counts_hbm, counts_ref, fetch_sems.at[0])
    table.start()
    parts = [None]
    for q in range(1, len(SHARES)):
        span = slice(spans[q].start - HELD, spans[q].stop - HELD)
        part = pltpu.make_async_copy(
            receive_hbm.at[spans[q]], receive_ref.at[span], fetch_sems.at[q]
        )
        part.start()
        parts.append(part)
    wide_ref[...] = rows_ref[...].astype(jnp.float32)
    for p in range(positions):
        v = wide_ref[pl.ds(p, directions, stride=positions), :].astype(jnp.bfloat16)
        doubled_ref[0:directions, p * 128 : (p + 1) * 128] = v
        doubled_ref[directions:doubled, p * 128 : (p + 1) * 128] = quarter(v)
    table.wait()
    offset, count = own_range(counts_ref)
    for slot in range(positions):

        @pl.when(slot >= count)
        def _():
            fields_ref[slot * children : (slot + 1) * children] = jnp.zeros(
                (children, unknowns, 128), jnp.bfloat16
            )

    stores = []
    for q, octants in enumerate(SHARES):
        base = spans[q].start
        if q:
            parts[q].wait()
        held = receive_ref[base - HELD : base - HELD + octants] if q else held_ref[...]
        lines = held.reshape(octants * unknowns, doubled)
        far = jnp.dot(lines, doubled_ref[...], preferred_element_type=jnp.float32)
        for p in range(positions):
            slot = p - offset

            @pl.when(jnp.logical_and(slot >= 0, slot < count))
            def _():
                for c in range(octants):
                    leaf = slot * children + base + c
                    part = far[c * unknowns : (c + 1) * unknowns, p * 128 : (p + 1) * 128]
                    fields_ref[leaf] = (part + near_ref[leaf]).astype(jnp.bfloat16)

        for slot in range(positions):
            span = pl.ds(slot * children + base, octants)
            store = pltpu.make_async_copy(
                fields_ref.at[span], out_hbm.at[span], store_sems.at[q, slot]
            )
            store.start()
            stores.append(store)
    for store in stores:
        store.wait()


def absorb(counts, rows, held, receive, near_field):
    children, _, doubled = receive.shape
    positions = near_field.shape[0] // children
    steps = len(SHARES)
    vmem = pl.BlockSpec(memory_space=pltpu.VMEM)
    hbm = pl.BlockSpec(memory_space=pltpu.HBM)
    return pl.pallas_call(
        absorb_kernel,
        in_specs=[hbm, vmem, vmem, vmem, hbm],
        out_specs=hbm,
        scratch_shapes=[
            pltpu.SMEM(counts.shape, counts.dtype),
            pltpu.VMEM(rows.shape, jnp.float32),
            pltpu.VMEM((doubled, positions * 128), jnp.bfloat16),
            pltpu.VMEM((children - HELD,) + receive.shape[1:], receive.dtype),
            pltpu.VMEM(near_field.shape, jnp.bfloat16),
            pltpu.SemaphoreType.DMA((steps,)),
            pltpu.SemaphoreType.DMA((steps, positions)),
        ],
        out_shape=jax.ShapeDtypeStruct(near_field.shape, jnp.bfloat16),
        compiler_params=pltpu.CompilerParams(vmem_limit_bytes=24 * MIB),
        name="absorb",
    )(counts, rows, near_field, held, receive)


def in_hbm(array):
    return pltpu.with_memory_space_constraint(array, pltpu.HBM)


def swap(rows, positions):
    channels = rows.shape[-1]
    shaped = rows.reshape(-1, positions, channels)
    return lax.all_to_all(shaped, AXES, 0, 0, tiled=True).reshape(-1, channels)


def body(
    currents, counts, near_source, near_blocks, aggregate, receive, translations, source_blocks
):
    slots = currents.shape[0]
    positions = slots // aggregate.shape[0]
    device = lax.axis_index(AXES)
    local = near_source - (device - 1) * slots
    mirrored = local + 2 * slots - 2 * slots * (local // slots)
    local = jnp.where(device % 2 == 1, mirrored, local)
    count = lax.axis_size("near")
    inner = [(i, i + 1) for i in range(1, count - 1, 2)]
    outer = [(i, i + 1) for i in range(0, count, 2)]
    across = lax.ppermute(currents, "near", inner + [(j, i) for i, j in inner])
    partner = lax.ppermute(currents, "near", outer + [(j, i) for i, j in outer])

    patterns = radiate(in_hbm(counts), in_hbm(currents), in_hbm(aggregate))
    gathered = swap(patterns, positions)
    incoming = translate(in_hbm(source_blocks), gathered, translations, positions)
    returned = swap(incoming, positions)

    local, _ = lax.optimization_barrier((local, incoming))
    near_field, held = near(
        local, across, in_hbm(currents), partner, in_hbm(near_blocks), in_hbm(receive)
    )
    return absorb(in_hbm(counts), returned, held, in_hbm(receive), near_field)


def solution(mesh):
    spread = P(AXES, None, None)
    return jax.shard_map(
        body,
        mesh=mesh,
        in_specs=(
            spread,
            P(),
            P(AXES, None),
            P(AXES, None, None, None),
            P(),
            P(),
            P(None, None, AXES, None, None),
            P(),
        ),
        out_specs=spread,
        check_vma=False,
    )
```
